32 devices in a mesh: groups: 2 (over y), wide: 16 (over z, x, core).
Axes of the slice: x: 2, y: 2, z: 4, core: 2. Of those that a mesh axis runs over, the one named last changes fastest.
Arguments:
- fields: bfloat16 [32, 512], P(('groups', 'wide')), parts along dimension 0, may hold values from -6 to 6
- chol: bfloat16 [512, 1024, 1024], P(None, 'wide'), may hold values from -0.01171875 to 0.01171875
- orbitals: bfloat16 [32, 1024, 256], P(('groups', 'wide')), parts along dimension 0, may hold values from -6 to 6
- trial: bfloat16 [1024, 256], replicated, may hold values from -0.5 to 0.5
Outputs:
- new_orbitals: bfloat16 [32, 1024, 256], P(('groups', 'wide')), parts along dimension 0
- force_bias: float32 [32, 2, 512], P(('groups', 'wide')), parts along dimension 0
The draws below stay inside these ranges and needn't reach their ends.
There are 2 independent parts, one for each index of `groups`. The reference program is written for one: setup_inputs(seed, part) draws one part's arguments, and reference() takes and returns one part's arrays. A program takes and returns all parts, laid end to end along the dimension named above; an argument that names none is the same for every part. Nothing has to cross between parts.
All inputs are finite; a program needn't handle non-finite values.
Results may differ from the reference program's by a relative error of at most 0.0075.
Values may be sent and summed in bfloat16 or wider, within the bound.
No kernel may reach another device: no remote copies, remote signals or barrier semaphores. Data moves between devices by JAX's collectives and lax.ppermute only.
A program may use at most 192 MiB of HBM per device.

```python
import jax
import jax.numpy as jnp
from jax import lax

N = 1024
NOCC = 128
NG = 512
TAYLOR = 4
WALKERS = 16


def level_of(key, extent, pieces, least, top_value):
    factor_of = 1.0
    for dim, parts in pieces:
        steps = jax.random.uniform(jax.random.fold_in(jax.random.fold_in(key, 6), dim), (parts,), jnp.float32, least / len(pieces), top_value / len(pieces))
        factor_of = factor_of * jnp.repeat(jnp.exp(steps), extent[dim] // parts).reshape((-1,) + (1,) * (len(extent) - 1 - dim))
    return factor_of


def bell_draw(rng, dims, scale, bound, split=(), kind=jnp.bfloat16):
    loudness = level_of(rng, dims, split, -0.22, 0.18) if split else 1.0
    entries = jax.random.normal(rng, dims, jnp.float32) * scale * loudness
    return jnp.minimum(jnp.maximum(entries, -bound), bound).astype(kind)


def setup_inputs(seed: int = 0, part: int = 0) -> dict:
    streams_of = jax.random.split(jax.random.key(seed), 5)
    part_keys = jax.random.split(jax.random.fold_in(streams_of[4], part), 5)
    fields = bell_draw(part_keys[0], (WALKERS, NG), 1.0, 6.0, ((0, 16),))
    chol = bell_draw(streams_of[1], (NG, N, N), (N * NG // 2) ** -0.5, 0.01171875, ((1, 16),))
    orbitals = bell_draw(part_keys[2], (WALKERS, N, 2 * NOCC), 1.0, 6.0, ((0, 16),))
    trial = bell_draw(streams_of[3], (N, 2 * NOCC), NOCC ** -0.5, 0.5)
    return {"fields": fields, "chol": chol, "orbitals": orbitals, "trial": trial}


def reference(fields, chol, orbitals, trial):
    chol_flat = chol.reshape(NG, N * N)
    generator = jnp.dot(fields, chol_flat, preferred_element_type=jnp.float32).astype(jnp.bfloat16).reshape(WALKERS, N, N)
    trial_real = trial[:, :NOCC].T
    trial_imag = trial[:, NOCC:].T
    mixer = jnp.concatenate([jnp.concatenate([trial_real, -trial_imag], axis=1), jnp.concatenate([trial_imag, trial_real], axis=1)], axis=0)

    def propagate(inputs):
        gen_walker, orb_walker = inputs
        total = orb_walker.astype(jnp.float32)
        operand = orb_walker
        for order in range(1, TAYLOR + 1):
            product = jnp.dot(gen_walker, operand, preferred_element_type=jnp.float32)
            term = jnp.concatenate([-product[:, NOCC:], product[:, :NOCC]], axis=1) / order
            total = total + term
            operand = term.astype(jnp.bfloat16)
        fresh = total.astype(jnp.bfloat16)
        green = jnp.dot(fresh, mixer, preferred_element_type=jnp.float32).astype(jnp.bfloat16)
        paired = jnp.stack([green[:, :N].reshape(-1), green[:, N:].reshape(-1)], axis=0)
        return fresh, paired

    new_orbitals, greens = lax.map(propagate, (generator, orbitals))
    greens = greens.reshape(WALKERS * 2, N * N)
    bias = jnp.dot(greens, chol_flat.T, preferred_element_type=jnp.float32)
    force_bias = bias.reshape(WALKERS, 2, NG)
    return new_orbitals, force_bias
```

```python
import functools

import jax
import jax.numpy as jnp
from jax import lax
from jax.experimental import pallas as pl
from jax.experimental.pallas import tpu as pltpu
from jax.sharding import PartitionSpec as P

TAYLOR = 4
RI = 8
BF16 = jnp.bfloat16
F32 = jnp.float32


def expand_kernel(f_ref, o_ref):
    walkers, vectors = f_ref.shape
    lane = lax.broadcasted_iota(jnp.int32, (128, 128 * RI), 1)
    row = lax.broadcasted_iota(jnp.int32, (128, 128 * RI), 0)
    repeat = (lane // RI == row).astype(F32).astype(BF16)
    sub = lax.broadcasted_iota(jnp.int32, (RI, 128 * RI), 0)
    keep = lax.broadcasted_iota(jnp.int32, (RI, 128 * RI), 1) % RI == sub
    for b in range(vectors // 128):
        v = jnp.dot(f_ref[:, b * 128 : (b + 1) * 128], repeat, preferred_element_type=F32)
        e = jnp.where(keep[None], v[:, None, :], 0.0)
        o_ref[:, b * 128 * RI : (b + 1) * 128 * RI] = e.reshape(walkers * RI, 128 * RI).astype(BF16)


def expand(f):
    w, g = f.shape
    return pl.pallas_call(
        expand_kernel,
        out_shape=jax.ShapeDtypeStruct((w * RI, g * RI), BF16),
        cost_estimate=pl.CostEstimate(flops=2 * w * g * 128 * RI, bytes_accessed=w * g * RI * RI * 2, transcendentals=0),
        name="expand",
    )(f)


def gen_kernel(fk_ref, x_ref, o_ref):
    vectors, _, n = x_ref.shape
    x = x_ref[...].reshape(vectors * RI, n)
    part = jnp.dot(fk_ref[...], x, preferred_element_type=F32)
    o_ref[...] = part.reshape(o_ref.shape).astype(BF16)


def gen(fk, chol, first, count):
    vectors, _, n = chol.shape
    w = fk.shape[0] // RI
    wb = min(w, 32)
    return pl.pallas_call(
        gen_kernel,
        grid=(count, w // wb),
        in_specs=[
            pl.BlockSpec((wb * RI, vectors * RI), lambda i, k: (k, 0)),
            pl.BlockSpec((vectors, RI, n), lambda i, k: (0, first + i, 0)),
        ],
        out_specs=pl.BlockSpec((wb, RI, n), lambda i, k: (k, i, 0)),
        out_shape=jax.ShapeDtypeStruct((w, count * RI, n), BF16),
        cost_estimate=pl.CostEstimate(
            flops=2 * w * RI * vectors * count * RI * n, bytes_accessed=vectors * count * RI * n * 2, transcendentals=0
        ),
        name=f"gen_{first}_{count}",
    )(fk, chol)


def half_kernel(t_ref, x_ref, o_ref):
    vectors, _, n = x_ref.shape
    x = x_ref[...].reshape(vectors * RI, n)
    p = jnp.dot(x, t_ref[...], preferred_element_type=F32)
    o_ref[...] = p.reshape(o_ref.shape).astype(BF16)


def half(trial, chol, first, count):
    vectors, _, n = chol.shape
    cols = trial.shape[1]
    return pl.pallas_call(
        half_kernel,
        grid=(count,),
        in_specs=[
            pl.BlockSpec((n, cols), lambda i: (0, 0)),
            pl.BlockSpec((vectors, RI, n), lambda i: (0, first + i, 0)),
        ],
        out_specs=pl.BlockSpec((vectors, RI, cols), lambda i: (0, 0, i)),
        out_shape=jax.ShapeDtypeStruct((vectors, RI, count * cols), BF16),
        cost_estimate=pl.CostEstimate(
            flops=2 * vectors * count * RI * n * cols,
            bytes_accessed=vectors * count * RI * (n + cols) * 2,
            transcendentals=0,
        ),
        name=f"half_{first}_{count}",
    )(trial, chol)


def taylor_kernel(*refs, counts):
    g_refs = refs[: len(counts)]
    q0_ref, new_ref, send_ref, total, even, odd = refs[len(counts) :]
    n, cols = q0_ref.shape
    nocc = cols // 2
    owners = g_refs[0].shape[0]
    rows = n // owners
    total[...] = q0_ref[...].astype(F32).reshape(owners, rows, cols)
    source = q0_ref
    for order in range(1, TAYLOR + 1):
        target = (even, odd)[order % 2]
        q = source[...].reshape(n, cols)
        start = 0
        for g_ref, count in zip(g_refs, counts):
            size = count * RI
            p = jnp.dot(g_ref[...].reshape(owners * size, n), q, preferred_element_type=F32)
            p = p.reshape(owners, size, cols) * (1.0 / order)
            term = jnp.concatenate([-p[:, :, nocc:], p[:, :, :nocc]], axis=2)
            total[:, start : start + size] += term
            if order < TAYLOR:
                target[:, start : start + size] = term.astype(BF16)
            start += size
        source = target
    fresh = total[...].astype(BF16)
    new_ref[...] = fresh.reshape(n, cols)
    for b in range(rows // RI):
        send_ref[:, :, b * cols : (b + 1) * cols] = fresh[:, b * RI : (b + 1) * RI]


def taylor(parts, counts, orbitals):
    n, cols = orbitals.shape
    owners = parts[0].shape[0]
    rows = n // owners
    return pl.pallas_call(
        functools.partial(taylor_kernel, counts=counts),
        out_shape=[
            jax.ShapeDtypeStruct((n, cols), BF16),
            jax.ShapeDtypeStruct((owners, RI, rows // RI * cols), BF16),
        ],
        scratch_shapes=[
            pltpu.VMEM((owners, rows, cols), F32),
            pltpu.VMEM((owners, rows, cols), BF16),
            pltpu.VMEM((owners, rows, cols), BF16),
        ],
        cost_estimate=pl.CostEstimate(flops=2 * TAYLOR * n * n * cols, bytes_accessed=n * (n + 3 * cols) * 2, transcendentals=0),
        name="taylor",
    )(*parts, orbitals)


def bias_kernel(*refs, counts):
    n_ref = refs[0]
    h_refs = refs[1 : 1 + len(counts)]
    o_ref, pair = refs[1 + len(counts) :]
    w, _, depth = n_ref.shape
    cols = depth // sum(counts)
    nocc = cols // 2

    @pl.when(pl.program_id(1) == 0)
    def _():
        v = n_ref[...]
        pair[:, 0] = v
        for b in range(depth // cols):
            s = b * cols
            pair[:, 1, :, s : s + nocc] = v[:, :, s + nocc : s + cols]
            pair[:, 1, :, s + nocc : s + cols] = -v[:, :, s : s + nocc]

    both = pair[...].reshape(w * 2 * RI, depth)
    size = h_refs[0].shape[0]
    out = None
    start = 0
    for h_ref, count in zip(h_refs, counts):
        wide = count * cols
        h = h_ref[...].reshape(size * RI, wide)
        part = lax.dot_general(
            h, both[:, start : start + wide], (((1,), (1,)), ((), ())), preferred_element_type=F32
        )
        out = part if out is None else out + part
        start += wide
    lanes = w * 2 * RI
    sub = lax.broadcasted_iota(jnp.int32, (RI, lanes), 0)
    keep = lax.broadcasted_iota(jnp.int32, (RI, lanes), 1) % RI == sub
    out = jnp.where(keep[None], out.reshape(size, RI, lanes), 0.0).sum(axis=1)
    o_ref[...] = out.T.reshape(w * 2, RI, size).sum(axis=1)


def bias(rows, halves, counts):
    w, _, depth = rows.shape
    vectors = halves[0].shape[0]
    size = min(vectors, 256)
    wb = min(w, 16)
    return pl.pallas_call(
        functools.partial(bias_kernel, counts=counts),
        grid=(w // wb, vectors // size),
        in_specs=[pl.BlockSpec((wb, RI, depth), lambda k, i: (k, 0, 0))]
        + [pl.BlockSpec((size, RI, h.shape[2]), lambda k, i: (i, 0, 0)) for h in halves],
        out_specs=pl.BlockSpec((wb * 2, size), lambda k, i: (k, i)),
        out_shape=jax.ShapeDtypeStruct((w * 2, vectors), F32),
        scratch_shapes=[pltpu.VMEM((wb, 2, RI, depth), BF16)],
        cost_estimate=pl.CostEstimate(
            flops=2 * vectors * RI * depth * w * 2 * RI, bytes_accessed=vectors * RI * depth * 2, transcendentals=0
        ),
        name="bias",
    )(rows, *halves)


def splits(groups):
    first = max(1, groups // 4)
    return (first, groups - first) if groups > first else (groups,)


def exchange(v):
    return lax.all_to_all(v, "wide", split_axis=0, concat_axis=0, tiled=True)


def per_device(fields, chol, orbitals, trial):
    owners = lax.axis_size("wide")
    vectors, rows, n = chol.shape
    counts = splits(rows // RI)
    all_fields = exchange(jnp.broadcast_to(fields, (owners,) + fields.shape[1:]))
    spread = expand(all_fields)
    parts = []
    start = 0
    for count in counts:
        parts.append(exchange(gen(spread, chol, start, count)))
        start += count
    halves = []
    start = 0
    for count in counts:
        halves.append(half(trial, chol, start, count))
        start += count
    fresh, send = taylor(parts, counts, orbitals[0])
    partial = bias(exchange(send), halves, counts)
    mine = exchange(partial.reshape(owners, 2, vectors))
    return fresh[None], mine.sum(axis=0, keepdims=True)


def solution(mesh):
    in_specs = (
        P(("groups", "wide"), None),
        P(None, "wide", None),
        P(("groups", "wide"), None, None),
        P(),
    )
    out_specs = (P(("groups", "wide"), None, None), P(("groups", "wide"), None, None))
    return jax.shard_map(
        per_device, mesh=mesh, in_specs=in_specs, out_specs=out_specs, check_vma=False
    )
```

```python
import functools

import jax
import jax.numpy as jnp
from jax import lax
from jax.experimental import pallas as pl
from jax.experimental.pallas import tpu as pltpu
from jax.sharding import PartitionSpec as P

TAYLOR = 4
RI = 8
WB = 16
BF16 = jnp.bfloat16
F32 = jnp.float32
MIB = 1 << 20
VMEM = pl.BlockSpec(memory_space=pltpu.VMEM)
HBM = pl.BlockSpec(memory_space=pltpu.HBM)


def grant(mib):
    return pltpu.CompilerParams(vmem_limit_bytes=mib * MIB)


def copies(fields, owners):
    def kernel(f_ref, o_ref):
        o_ref[...] = jnp.broadcast_to(f_ref[...].astype(F32)[:, None, :], o_ref.shape).astype(BF16)

    return pl.pallas_call(
        kernel,
        in_specs=[VMEM],
        out_specs=VMEM,
        out_shape=jax.ShapeDtypeStruct((owners, RI, fields.shape[1]), BF16),
        compiler_params=grant(4),
        name="copies",
    )(fields)


def expand(f):
    w, _, g = f.shape

    def kernel(f_ref, o_ref):
        fields = f_ref[...].astype(F32)[:, 0, :].astype(BF16)
        lane = lax.broadcasted_iota(jnp.int32, (128, 128 * RI), 1)
        row = lax.broadcasted_iota(jnp.int32, (128, 128 * RI), 0)
        repeat = (lane // RI == row).astype(F32).astype(BF16)
        sub = lax.broadcasted_iota(jnp.int32, (RI, 128 * RI), 0)
        keep = lax.broadcasted_iota(jnp.int32, (RI, 128 * RI), 1) % RI == sub
        for b in range(g // 128):
            v = jnp.dot(fields[:, b * 128 : (b + 1) * 128], repeat, preferred_element_type=F32)
            e = jnp.where(keep[None], v[:, None, :], 0.0)
            o_ref[:, b * 128 * RI : (b + 1) * 128 * RI] = e.reshape(w * RI, 128 * RI).astype(BF16)

    return pl.pallas_call(
        kernel,
        in_specs=[VMEM],
        out_specs=VMEM,
        out_shape=jax.ShapeDtypeStruct((w * RI, g * RI), BF16),
        compiler_params=grant(16),
        cost_estimate=pl.CostEstimate(flops=2 * w * g * 128 * RI, bytes_accessed=w * g * RI * RI * 2, transcendentals=0),
        name="expand",
    )(f)


def gen(fk, chol, first, count):
    vectors, _, n = chol.shape
    w = fk.shape[0] // RI
    wb = min(w, WB)
    pieces, slots = 8, 8
    size = vectors // pieces

    def kernel(fk_ref, c_ref, o_ref, held, done, acc, in_sems, out_sems):
        def fetch(group, piece, slot):
            return pltpu.make_async_copy(
                c_ref.at[pl.ds(piece * size, size), pl.ds(pl.multiple_of((first + group) * RI, RI), RI), :],
                held.at[slot],
                in_sems.at[slot],
            )

        def put(group, slot):
            return pltpu.make_async_copy(
                done.at[slot], o_ref.at[:, pl.ds(pl.multiple_of(group * RI, RI), RI), :], out_sems.at[slot]
            )

        for p in range(slots - 1):
            fetch(0, p, p).start()

        def body(group, _):
            for p in range(pieces):
                fetch(group, p, p).wait()
                ahead = (p + slots - 1) % slots
                if p == 0:
                    fetch(group, ahead, ahead).start()
                else:

                    @pl.when(group + 1 < count)
                    def _():
                        fetch(group + 1, ahead, ahead).start()

                x = held[p].reshape(size * RI, n)
                for k in range(w // wb):
                    r = slice(k * wb * RI, (k + 1) * wb * RI)
                    part = jnp.dot(fk_ref[r, p * size * RI : (p + 1) * size * RI], x, preferred_element_type=F32)
                    if p == 0:
                        acc[r] = part
                    else:
                        acc[r] += part
            slot = lax.rem(group, 2)

            @pl.when(group >= 2)
            def _():
                put(group - 2, slot).wait()

            done[slot] = acc[...].reshape(w, RI, n).astype(BF16)
            put(group, slot).start()
            return 0

        lax.fori_loop(0, count, body, 0)
        for group in range(max(0, count - 2), count):
            put(group, group % 2).wait()

    return pl.pallas_call(
        kernel,
        in_specs=[VMEM, HBM],
        out_specs=HBM,
        out_shape=jax.ShapeDtypeStruct((w, count * RI, n), BF16),
        scratch_shapes=[
            pltpu.VMEM((slots, size, RI, n), BF16),
            pltpu.VMEM((2, w, RI, n), BF16),
            pltpu.VMEM((w * RI, n), F32),
            pltpu.SemaphoreType.DMA((slots,)),
            pltpu.SemaphoreType.DMA((2,)),
        ],
        cost_estimate=pl.CostEstimate(
            flops=2 * w * RI * vectors * count * RI * n, bytes_accessed=vectors * count * RI * n * 2, transcendentals=0
        ),
        compiler_params=grant(16 + w // 4),
    )(fk, chol)


def half(trial, chol, first, count):
    vectors, _, n = chol.shape
    cols = trial.shape[1]

    def kernel(t_ref, x_ref, o_ref):
        x = x_ref[...].reshape(vectors * RI, n)
        p = jnp.dot(x, t_ref[...], preferred_element_type=F32)
        o_ref[...] = p.reshape(o_ref.shape).astype(BF16)

    return pl.pallas_call(
        kernel,
        grid=(count,),
        in_specs=[
            pl.BlockSpec((n, cols), lambda i: (0, 0)),
            pl.BlockSpec((vectors, RI, n), lambda i: (0, first + i, 0)),
        ],
        out_specs=pl.BlockSpec((vectors, RI, cols), lambda i: (0, 0, i)),
        out_shape=jax.ShapeDtypeStruct((vectors, RI, count * cols), BF16),
        cost_estimate=pl.CostEstimate(
            flops=2 * vectors * count * RI * n * cols,
            bytes_accessed=vectors * count * RI * (n + cols) * 2,
            transcendentals=0,
        ),
        compiler_params=grant(56),
    )(trial, chol)


def taylor_kernel(*refs, counts):
    g_refs = refs[: len(counts)]
    q0_ref, new_ref, send_ref, total, even, odd = refs[len(counts) :]
    n, cols = q0_ref.shape
    nocc = cols // 2
    owners = g_refs[0].shape[0]
    rows = n // owners
    total[...] = q0_ref[...].astype(F32).reshape(owners, rows, cols)
    source = q0_ref
    for order in range(1, TAYLOR + 1):
        target = (even, odd)[order % 2]
        q = source[...].reshape(n, cols)
        start = 0
        for g_ref, count in zip(g_refs, counts):
            size = count * RI
            p = jnp.dot(g_ref[...].reshape(owners * size, n), q, preferred_element_type=F32)
            p = p.reshape(owners, size, cols) * (1.0 / order)
            term = jnp.concatenate([-p[:, :, nocc:], p[:, :, :nocc]], axis=2)
            total[:, start : start + size] += term
            if order < TAYLOR:
                target[:, start : start + size] = term.astype(BF16)
            start += size
        source = target
    fresh = total[...].astype(BF16)
    new_ref[...] = fresh.reshape(n, cols)
    for b in range(rows // RI):
        send_ref[:, :, b * cols : (b + 1) * cols] = fresh[:, b * RI : (b + 1) * RI]


def taylor(parts, counts, orbitals):
    n, cols = orbitals.shape
    owners = parts[0].shape[0]
    rows = n // owners
    return pl.pallas_call(
        functools.partial(taylor_kernel, counts=counts),
        in_specs=[VMEM] * (len(parts) + 1),
        out_specs=[VMEM, VMEM],
        out_shape=[
            jax.ShapeDtypeStruct((n, cols), BF16),
            jax.ShapeDtypeStruct((owners, RI, rows // RI * cols), BF16),
        ],
        scratch_shapes=[
            pltpu.VMEM((owners, rows, cols), F32),
            pltpu.VMEM((owners, rows, cols), BF16),
            pltpu.VMEM((owners, rows, cols), BF16),
        ],
        cost_estimate=pl.CostEstimate(flops=2 * TAYLOR * n * n * cols, bytes_accessed=n * (n + 3 * cols) * 2, transcendentals=0),
        compiler_params=grant(12),
        name="taylor",
    )(*parts, orbitals)


def bias_kernel(*refs, counts):
    n_ref = refs[0]
    h_refs = refs[1 : 1 + len(counts)]
    o_ref, pair, sems = refs[1 + len(counts) : 4 + len(counts)]
    held = refs[4 + len(counts) :]
    w, _, depth = n_ref.shape
    wb = min(w, WB)
    cols = depth // sum(counts)
    nocc = cols // 2
    vectors = h_refs[0].shape[0]
    pieces = sems.shape[0]
    size = vectors // pieces
    lanes = wb * 2 * RI
    sub = lax.broadcasted_iota(jnp.int32, (RI, lanes), 0)
    keep = lax.broadcasted_iota(jnp.int32, (RI, lanes), 1) % RI == sub

    def fetch(piece, c):
        at = pl.ds(piece * size, size)
        return pltpu.make_async_copy(h_refs[c].at[at], held[c].at[at], sems.at[piece, c])

    for piece in range(pieces):
        for c in range(len(counts)):
            fetch(piece, c).start()

    def block(k, ready):
        for b in range(depth // cols):
            s = b * cols
            real = n_ref[pl.ds(k * wb, wb), :, s : s + cols].astype(F32)
            imag = jnp.concatenate([real[:, :, nocc:], -real[:, :, :nocc]], axis=2)
            pair[:, s : s + cols] = jnp.stack([real, imag], axis=1).reshape(lanes, cols).astype(BF16)
        sums = []
        for piece in range(pieces):
            out = None
            start = 0
            for c, count in enumerate(counts):
                if ready is None:
                    fetch(piece, c).wait()
                wide = count * cols
                h = held[c][piece * size : (piece + 1) * size].reshape(size * RI, wide)
                part = lax.dot_general(
                    h, pair[:, start : start + wide], (((1,), (1,)), ((), ())), preferred_element_type=F32
                )
                out = part if out is None else out + part
                start += wide
            sums.append(jnp.where(keep[None], out.reshape(size, RI, lanes), 0.0).sum(axis=1))
            if len(sums) * size == 128:
                done = jnp.concatenate(sums, axis=0) if len(sums) > 1 else sums[0]
                v = (piece + 1) * size - 128
                o_ref[pl.ds(k * wb, wb), :, v : v + 128] = (
                    done.T.reshape(wb * 2, RI, 128).sum(axis=1).reshape(wb, 2, 128)
                )
                sums = []

    block(0, None)
    if w > wb:
        pl.loop(1, w // wb)(lambda k: block(k, True))


def bias(rows, halves, counts):
    w, _, depth = rows.shape
    vectors = halves[0].shape[0]
    wb = min(w, WB)
    return pl.pallas_call(
        functools.partial(bias_kernel, counts=counts),
        in_specs=[VMEM] + [HBM] * len(halves),
        out_specs=VMEM,
        out_shape=jax.ShapeDtypeStruct((w, 2, vectors), F32),
        scratch_shapes=[
            pltpu.VMEM((wb * 2 * RI, depth), BF16),
            pltpu.SemaphoreType.DMA((vectors // 64, len(halves))),
        ]
        + [pltpu.VMEM(h.shape, BF16) for h in halves],
        cost_estimate=pl.CostEstimate(
            flops=2 * vectors * RI * depth * w * 2 * RI, bytes_accessed=vectors * RI * depth * 2, transcendentals=0
        ),
        compiler_params=grant(56),
        name="bias",
    )(rows, *halves)


def splits(groups):
    first = max(1, 3 * groups // 8)
    return (first, groups - first) if groups > first else (groups,)


def exchange(v):
    return lax.all_to_all(v, "wide", split_axis=0, concat_axis=0, tiled=True)


def per_device(fields, chol, orbitals, trial):
    owners = lax.axis_size("wide")
    rows = chol.shape[1]
    counts = splits(rows // RI)
    everyone = exchange(copies(fields, owners))
    spread = expand(everyone)
    parts = [exchange(gen(spread, chol, 0, counts[0]))]
    if len(counts) > 1:
        more = gen(spread, chol, counts[0], counts[1])
        parts.append(exchange(more))
    halves = []
    start = 0
    for count in counts:
        halves.append(half(trial, chol, start, count))
        start += count
    fresh, send = taylor(parts, counts, orbitals[0])
    rows_all = exchange(send)
    mine = exchange(bias(rows_all, halves, counts))
    return fresh[None], mine.sum(axis=0, keepdims=True)


def solution(mesh):
    in_specs = (
        P(("groups", "wide"), None),
        P(None, "wide", None),
        P(("groups", "wide"), None, None),
        P(),
    )
    out_specs = (P(("groups", "wide"), None, None), P(("groups", "wide"), None, None))
    return jax.shard_map(
        per_device, mesh=mesh, in_specs=in_specs, out_specs=out_specs, check_vma=False
    )
```

```python
import functools

import jax
import jax.numpy as jnp
from jax import lax
from jax.experimental import pallas as pl
from jax.experimental.pallas import tpu as pltpu
from jax.sharding import PartitionSpec as P

TAYLOR = 4
RI = 8
WB = 16
BF16 = jnp.bfloat16
F32 = jnp.float32
MIB = 1 << 20
VMEM = pl.BlockSpec(memory_space=pltpu.VMEM)
HBM = pl.BlockSpec(memory_space=pltpu.HBM)


def grant(mib):
    return pltpu.CompilerParams(vmem_limit_bytes=mib * MIB)


def copies(fields, owners):
    def kernel(f_ref, o_ref):
        o_ref[...] = jnp.broadcast_to(f_ref[...].astype(F32)[:, None, :], o_ref.shape).astype(BF16)

    return pl.pallas_call(
        kernel,
        in_specs=[VMEM],
        out_specs=VMEM,
        out_shape=jax.ShapeDtypeStruct((owners, RI, fields.shape[1]), BF16),
        compiler_params=grant(4),
        name="copies",
    )(fields)


def expand(f):
    w, _, g = f.shape

    def kernel(f_ref, o_ref):
        fields = f_ref[...].astype(F32)[:, 0, :].astype(BF16)
        lane = lax.broadcasted_iota(jnp.int32, (128, 128 * RI), 1)
        row = lax.broadcasted_iota(jnp.int32, (128, 128 * RI), 0)
        repeat = (lane // RI == row).astype(F32).astype(BF16)
        sub = lax.broadcasted_iota(jnp.int32, (RI, 128 * RI), 0)
        keep = lax.broadcasted_iota(jnp.int32, (RI, 128 * RI), 1) % RI == sub
        for b in range(g // 128):
            v = jnp.dot(fields[:, b * 128 : (b + 1) * 128], repeat, preferred_element_type=F32)
            e = jnp.where(keep[None], v[:, None, :], 0.0)
            o_ref[:, b * 128 * RI : (b + 1) * 128 * RI] = e.reshape(w * RI, 128 * RI).astype(BF16)

    return pl.pallas_call(
        kernel,
        in_specs=[VMEM],
        out_specs=VMEM,
        out_shape=jax.ShapeDtypeStruct((w * RI, g * RI), BF16),
        compiler_params=grant(16),
        cost_estimate=pl.CostEstimate(flops=2 * w * g * 128 * RI, bytes_accessed=w * g * RI * RI * 2, transcendentals=0),
        name="expand",
    )(f)


def gen(fk, chol, trial, first, count, both):
    vectors, _, n = chol.shape
    cols = trial.shape[1]
    w = fk.shape[0] // RI
    wb = min(w, WB)
    pieces, slots = 8, 8
    size = vectors // pieces

    def kernel(fk_ref, c_ref, *refs):
        if both:
            t_ref, o_ref, h_ref, held, done, acc, in_sems, out_sems, side, side_sems = refs
        else:
            o_ref, held, done, acc, in_sems, out_sems = refs

        def fetch(group, piece, slot):
            return pltpu.make_async_copy(
                c_ref.at[pl.ds(piece * size, size), pl.ds(pl.multiple_of((first + group) * RI, RI), RI), :],
                held.at[slot],
                in_sems.at[slot],
            )

        def put(group, slot):
            return pltpu.make_async_copy(
                done.at[slot], o_ref.at[:, pl.ds(pl.multiple_of(group * RI, RI), RI), :], out_sems.at[slot]
            )

        def put_side(group, slot):
            return pltpu.make_async_copy(
                side.at[slot],
                h_ref.at[:, :, pl.ds(pl.multiple_of((first + group) * cols, cols), cols)],
                side_sems.at[slot],
            )

        for p in range(slots - 1):
            fetch(0, p, p).start()

        def body(group, with_side):
            for p in range(pieces):
                fetch(group, p, p).wait()
                ahead = (p + slots - 1) % slots
                if p == 0:
                    fetch(group, ahead, ahead).start()
                else:

                    @pl.when(group + 1 < count)
                    def _():
                        fetch(group + 1, ahead, ahead).start()

                x = held[p].reshape(size * RI, n)
                for k in range(w // wb):
                    r = slice(k * wb * RI, (k + 1) * wb * RI)
                    part = jnp.dot(fk_ref[r, p * size * RI : (p + 1) * size * RI], x, preferred_element_type=F32)
                    if p == 0:
                        acc[r] = part
                    else:
                        acc[r] += part
                if with_side:
                    product = jnp.dot(x, t_ref[...], preferred_element_type=F32)
                    side[group, p * size : (p + 1) * size] = product.reshape(size, RI, cols).astype(BF16)
            slot = lax.rem(group, 2)

            @pl.when(group >= 2)
            def _():
                put(group - 2, slot).wait()

            done[slot] = acc[...].reshape(w, RI, n).astype(BF16)
            put(group, slot).start()
            if with_side:
                put_side(group, group).start()

        if both:
            pl.loop(0, both)(lambda group: body(group, True))
        if both < count:
            pl.loop(both, count)(lambda group: body(group, False))
        for group in range(max(0, count - 2), count):
            put(group, group % 2).wait()
        for group in range(both):
            put_side(group, group).wait()

    rows_out = jax.ShapeDtypeStruct((w, count * RI, n), BF16)
    half_out = jax.ShapeDtypeStruct((vectors, RI, chol.shape[1] // RI * cols), BF16)
    out = pl.pallas_call(
        kernel,
        in_specs=[VMEM, HBM] + [VMEM] * bool(both),
        out_specs=[HBM, HBM] if both else HBM,
        out_shape=[rows_out, half_out] if both else rows_out,
        scratch_shapes=[
            pltpu.VMEM((slots, size, RI, n), BF16),
            pltpu.VMEM((2, w, RI, n), BF16),
            pltpu.VMEM((w * RI, n), F32),
            pltpu.SemaphoreType.DMA((slots,)),
            pltpu.SemaphoreType.DMA((2,)),
        ]
        + ([pltpu.VMEM((both, vectors, RI, cols), BF16), pltpu.SemaphoreType.DMA((both,))] if both else []),
        cost_estimate=pl.CostEstimate(
            flops=2 * w * RI * vectors * count * RI * n, bytes_accessed=vectors * count * RI * n * 2, transcendentals=0
        ),
        compiler_params=grant(56 if both else 16 + w // 4),
    )(fk, chol, *([trial] if both else []))
    return out if both else (out, None)


def half(trial, chol, some, skip):
    vectors, rows, n = chol.shape
    cols = trial.shape[1]
    groups = rows // RI
    start, stop = skip
    count = groups - (stop - start)

    def kernel(t_ref, x_ref, *refs):
        o_ref = refs[-1]
        x = x_ref[...].reshape(vectors * RI, n)
        p = jnp.dot(x, t_ref[...], preferred_element_type=F32)
        o_ref[...] = p.reshape(o_ref.shape).astype(BF16)

    def group(i):
        return jnp.where(i < start, i, i + (stop - start))

    held = some is not None
    return pl.pallas_call(
        kernel,
        grid=(count,),
        in_specs=[
            pl.BlockSpec((n, cols), lambda i: (0, 0)),
            pl.BlockSpec((vectors, RI, n), lambda i: (0, group(i), 0)),
        ]
        + [HBM] * held,
        out_specs=pl.BlockSpec((vectors, RI, cols), lambda i: (0, 0, group(i))),
        out_shape=jax.ShapeDtypeStruct((vectors, RI, groups * cols), BF16),
        input_output_aliases={2: 0} if held else {},
        cost_estimate=pl.CostEstimate(
            flops=2 * vectors * count * RI * n * cols,
            bytes_accessed=vectors * count * RI * (n + cols) * 2,
            transcendentals=0,
        ),
        compiler_params=grant(56),
        name="half",
    )(trial, chol, *([some] if held else []))


def taylor_kernel(*refs, counts):
    g_refs = refs[: len(counts)]
    q0_ref, half_ref, new_ref, send_ref, kept_ref, total, even, odd, sem = refs[len(counts) :]
    keep = pltpu.make_async_copy(half_ref.at[pl.ds(0, kept_ref.shape[0])], kept_ref, sem)
    keep.start()
    n, cols = q0_ref.shape
    nocc = cols // 2
    owners = g_refs[0].shape[0]
    rows = n // owners
    total[...] = q0_ref[...].astype(F32).reshape(owners, rows, cols)
    source = q0_ref
    for order in range(1, TAYLOR + 1):
        target = (even, odd)[order % 2]
        q = source[...].reshape(n, cols)
        start = 0
        for g_ref, count in zip(g_refs, counts):
            size = count * RI
            p = jnp.dot(g_ref[...].reshape(owners * size, n), q, preferred_element_type=F32)
            p = p.reshape(owners, size, cols) * (1.0 / order)
            term = jnp.concatenate([-p[:, :, nocc:], p[:, :, :nocc]], axis=2)
            total[:, start : start + size] += term
            if order < TAYLOR:
                target[:, start : start + size] = term.astype(BF16)
            start += size
        source = target
    fresh = total[...].astype(BF16)
    new_ref[...] = fresh.reshape(n, cols)
    for b in range(rows // RI):
        send_ref[:, :, b * cols : (b + 1) * cols] = fresh[:, b * RI : (b + 1) * RI]
    keep.wait()


def taylor(parts, counts, orbitals, halves):
    kept = (halves.shape[0] // 2,) + halves.shape[1:]
    n, cols = orbitals.shape
    owners = parts[0].shape[0]
    rows = n // owners
    return pl.pallas_call(
        functools.partial(taylor_kernel, counts=counts),
        in_specs=[VMEM] * (len(parts) + 1) + [HBM],
        out_specs=[VMEM] * 3,
        out_shape=[
            jax.ShapeDtypeStruct((n, cols), BF16),
            jax.ShapeDtypeStruct((owners, RI, rows // RI * cols), BF16),
            jax.ShapeDtypeStruct(kept, BF16),
        ],
        scratch_shapes=[
            pltpu.VMEM((owners, rows, cols), F32),
            pltpu.VMEM((owners, rows, cols), BF16),
            pltpu.VMEM((owners, rows, cols), BF16),
            pltpu.SemaphoreType.DMA,
        ],
        cost_estimate=pl.CostEstimate(flops=2 * TAYLOR * n * n * cols, bytes_accessed=n * (n + 3 * cols) * 2, transcendentals=0),
        compiler_params=grant(44),
        name="taylor",
    )(*parts, orbitals, halves)


def bias_kernel(*refs, cols):
    n_ref, k_ref, h_ref, o_ref, pair, rest, sems = refs
    w, _, depth = n_ref.shape
    vectors = h_ref.shape[0]
    wb = min(w, WB)
    nocc = cols // 2
    size = 128
    lanes = wb * 2 * RI
    sub = lax.broadcasted_iota(jnp.int32, (RI, lanes), 0)
    keep = lax.broadcasted_iota(jnp.int32, (RI, lanes), 1) % RI == sub
    kept = k_ref.shape[0]
    dmas = [
        pltpu.make_async_copy(h_ref.at[pl.ds(kept + v, size)], rest.at[pl.ds(v, size)], sems.at[v // size])
        for v in range(0, vectors - kept, size)
    ]
    for dma in dmas:
        dma.start()

    def block(k, fetched):
        for s in range(0, depth, cols):
            real = n_ref[pl.ds(k * wb, wb), :, s : s + cols].astype(F32)
            imag = jnp.concatenate([real[:, :, nocc:], -real[:, :, :nocc]], axis=2)
            pair[s : s + cols, :] = jnp.stack([real, imag], axis=1).reshape(lanes, cols).T.astype(BF16)
        for v in range(0, vectors, size):
            if v >= kept and not fetched:
                dmas[(v - kept) // size].wait()
            h = (k_ref[v : v + size] if v < kept else rest[v - kept : v - kept + size]).reshape(size * RI, depth)
            out = jnp.dot(h, pair[...], preferred_element_type=F32)
            out = jnp.where(keep[None], out.reshape(size, RI, lanes), 0.0).sum(axis=1)
            o_ref[pl.ds(k * wb, wb), :, v : v + size] = (
                out.T.reshape(wb * 2, RI, size).sum(axis=1).reshape(wb, 2, size)
            )

    block(0, False)
    if w > wb:
        pl.loop(1, w // wb)(lambda k: block(k, True))


def bias(rows, kept, halves, cols):
    w, _, depth = rows.shape
    vectors = halves.shape[0]
    wb = min(w, WB)
    return pl.pallas_call(
        functools.partial(bias_kernel, cols=cols),
        in_specs=[VMEM, VMEM, HBM],
        out_specs=VMEM,
        out_shape=jax.ShapeDtypeStruct((w, 2, vectors), F32),
        scratch_shapes=[
            pltpu.VMEM((depth, wb * 2 * RI), BF16),
            pltpu.VMEM((vectors - kept.shape[0],) + halves.shape[1:], BF16),
            pltpu.SemaphoreType.DMA(((vectors - kept.shape[0]) // 128,)),
        ],
        cost_estimate=pl.CostEstimate(
            flops=2 * vectors * RI * depth * w * 2 * RI, bytes_accessed=vectors * RI * depth * 2, transcendentals=0
        ),
        compiler_params=grant(44),
        name="bias",
    )(rows, kept, halves)


def splits(groups):
    first = max(1, 3 * groups // 8)
    return (first, groups - first) if groups > first else (groups,)


def exchange(v):
    return lax.all_to_all(v, "wide", split_axis=0, concat_axis=0, tiled=True)


def per_device(fields, chol, orbitals, trial):
    owners = lax.axis_size("wide")
    groups = chol.shape[1] // RI
    cols = trial.shape[1]
    counts = splits(groups)
    start = counts[0]
    stop = start + (min(2, counts[1]) if len(counts) > 1 else 0)
    everyone = exchange(copies(fields, owners))
    spread = expand(everyone)
    parts = [exchange(gen(spread, chol, trial, 0, counts[0], 0)[0])]
    some = None
    if len(counts) > 1:
        more, some = gen(spread, chol, trial, start, counts[1], stop - start)
        parts.append(exchange(more))
    halves = half(trial, chol, some, (start, stop))
    fresh, send, kept = taylor(parts, counts, orbitals[0], halves)
    rows_all = exchange(send)
    mine = exchange(bias(rows_all, kept, halves, cols))
    return fresh[None], mine.sum(axis=0, keepdims=True)


def solution(mesh):
    in_specs = (
        P(("groups", "wide"), None),
        P(None, "wide", None),
        P(("groups", "wide"), None, None),
        P(),
    )
    out_specs = (P(("groups", "wide"), None, None), P(("groups", "wide"), None, None))
    return jax.shard_map(
        per_device, mesh=mesh, in_specs=in_specs, out_specs=out_specs, check_vma=False
    )
```

```python
import functools

import jax
import jax.numpy as jnp
from jax import lax
from jax.experimental import pallas as pl
from jax.experimental.pallas import tpu as pltpu
from jax.sharding import PartitionSpec as P

TAYLOR = 4
RI = 8
WB = 16
BF16 = jnp.bfloat16
F32 = jnp.float32
MIB = 1 << 20
VMEM = pl.BlockSpec(memory_space=pltpu.VMEM)
HBM = pl.BlockSpec(memory_space=pltpu.HBM)


def grant(mib):
    return pltpu.CompilerParams(vmem_limit_bytes=mib * MIB)


def copies(fields, owners):
    def kernel(f_ref, o_ref):
        o_ref[...] = jnp.broadcast_to(f_ref[...].astype(F32)[:, None, :], o_ref.shape).astype(BF16)

    return pl.pallas_call(
        kernel,
        in_specs=[VMEM],
        out_specs=VMEM,
        out_shape=jax.ShapeDtypeStruct((owners, RI, fields.shape[1]), BF16),
        compiler_params=grant(4),
        name="copies",
    )(fields)


def expand(f):
    w, _, g = f.shape

    def kernel(f_ref, o_ref):
        fields = f_ref[...].astype(F32)[:, 0, :].astype(BF16)
        lane = lax.broadcasted_iota(jnp.int32, (128, 128 * RI), 1)
        row = lax.broadcasted_iota(jnp.int32, (128, 128 * RI), 0)
        repeat = (lane // RI == row).astype(F32).astype(BF16)
        sub = lax.broadcasted_iota(jnp.int32, (RI, 128 * RI), 0)
        keep = lax.broadcasted_iota(jnp.int32, (RI, 128 * RI), 1) % RI == sub
        for b in range(g // 128):
            v = jnp.dot(fields[:, b * 128 : (b + 1) * 128], repeat, preferred_element_type=F32)
            e = jnp.where(keep[None], v[:, None, :], 0.0)
            o_ref[:, b * 128 * RI : (b + 1) * 128 * RI] = e.reshape(w * RI, 128 * RI).astype(BF16)

    return pl.pallas_call(
        kernel,
        in_specs=[VMEM],
        out_specs=VMEM,
        out_shape=jax.ShapeDtypeStruct((w * RI, g * RI), BF16),
        compiler_params=grant(16),
        cost_estimate=pl.CostEstimate(flops=2 * w * g * 128 * RI, bytes_accessed=w * g * RI * RI * 2, transcendentals=0),
        name="expand",
    )(f)


def gen(fk, chol, trial, first, count, both):
    vectors, _, n = chol.shape
    cols = trial.shape[1]
    w = fk.shape[0] // RI
    wb = min(w, WB)
    pieces = 8
    size = vectors // pieces
    slots = 2 * pieces if both else pieces

    def kernel(fk_ref, c_ref, *refs):
        if both:
            t_ref, o_ref, h_ref, held, done, acc, in_sems, out_sems, side, side_sems = refs
        else:
            o_ref, held, done, acc, in_sems, out_sems = refs

        def fetch(group, piece, slot):
            return pltpu.make_async_copy(
                c_ref.at[pl.ds(piece * size, size), pl.ds(pl.multiple_of((first + group) * RI, RI), RI), :],
                held.at[slot],
                in_sems.at[slot],
            )

        def put(group, slot):
            return pltpu.make_async_copy(
                done.at[slot], o_ref.at[:, pl.ds(pl.multiple_of(group * RI, RI), RI), :], out_sems.at[slot]
            )

        def put_side(group, slot):
            return pltpu.make_async_copy(
                side.at[slot],
                h_ref.at[:, :, pl.ds(pl.multiple_of((first + group) * cols, cols), cols)],
                side_sems.at[slot],
            )

        def base(group):
            return lax.rem(group, 2) * pieces if both else 0

        for p in range(pieces - 1):
            fetch(0, p, p).start()

        def body(group, with_side):
            here, there = base(group), base(group + 1)
            for p in range(pieces):
                fetch(group, p, here + p).wait()
                if p == 0:
                    fetch(group, pieces - 1, here + pieces - 1).start()
                else:

                    @pl.when(group + 1 < count)
                    def _():
                        fetch(group + 1, p - 1, there + p - 1).start()

                x = held[here + p].reshape(size * RI, n)
                for k in range(w // wb):
                    r = slice(k * wb * RI, (k + 1) * wb * RI)
                    part = jnp.dot(fk_ref[r, p * size * RI : (p + 1) * size * RI], x, preferred_element_type=F32)
                    if p == 0:
                        acc[r] = part
                    else:
                        acc[r] += part
            if with_side:
                x = held[pl.ds(here, pieces)].reshape(vectors * RI, n)
                product = jnp.dot(x, t_ref[...], preferred_element_type=F32)
                side[group] = product.reshape(vectors, RI, cols).astype(BF16)
            slot = lax.rem(group, 2)

            @pl.when(group >= 2)
            def _():
                put(group - 2, slot).wait()

            done[slot] = acc[...].reshape(w, RI, n).astype(BF16)
            put(group, slot).start()
            if with_side:
                put_side(group, group).start()

        if both:
            pl.loop(0, both)(lambda group: body(group, True))
        if both < count:
            pl.loop(both, count)(lambda group: body(group, False))
        for group in range(max(0, count - 2), count):
            put(group, group % 2).wait()
        for group in range(both):
            put_side(group, group).wait()

    rows_out = jax.ShapeDtypeStruct((w, count * RI, n), BF16)
    half_out = jax.ShapeDtypeStruct((vectors, RI, chol.shape[1] // RI * cols), BF16)
    out = pl.pallas_call(
        kernel,
        in_specs=[VMEM, HBM] + [VMEM] * bool(both),
        out_specs=[HBM, HBM] if both else HBM,
        out_shape=[rows_out, half_out] if both else rows_out,
        scratch_shapes=[
            pltpu.VMEM((slots, size, RI, n), BF16),
            pltpu.VMEM((2, w, RI, n), BF16),
            pltpu.VMEM((w * RI, n), F32),
            pltpu.SemaphoreType.DMA((slots,)),
            pltpu.SemaphoreType.DMA((2,)),
        ]
        + ([pltpu.VMEM((both, vectors, RI, cols), BF16), pltpu.SemaphoreType.DMA((both,))] if both else []),
        cost_estimate=pl.CostEstimate(
            flops=2 * w * RI * vectors * count * RI * n, bytes_accessed=vectors * count * RI * n * 2, transcendentals=0
        ),
        compiler_params=grant(56 if both else 16 + w // 4),
    )(fk, chol, *([trial] if both else []))
    return out if both else (out, None)


def half(trial, chol, some, skip):
    vectors, rows, n = chol.shape
    cols = trial.shape[1]
    groups = rows // RI
    start, stop = skip
    count = groups - (stop - start)

    def kernel(t_ref, x_ref, *refs):
        o_ref = refs[-1]
        x = x_ref[...].reshape(vectors * RI, n)
        p = jnp.dot(x, t_ref[...], preferred_element_type=F32)
        o_ref[...] = p.reshape(o_ref.shape).astype(BF16)

    def group(i):
        return jnp.where(i < start, i, i + (stop - start))

    held = some is not None
    return pl.pallas_call(
        kernel,
        grid=(count,),
        in_specs=[
            pl.BlockSpec((n, cols), lambda i: (0, 0)),
            pl.BlockSpec((vectors, RI, n), lambda i: (0, group(i), 0)),
        ]
        + [HBM] * held,
        out_specs=pl.BlockSpec((vectors, RI, cols), lambda i: (0, 0, group(i))),
        out_shape=jax.ShapeDtypeStruct((vectors, RI, groups * cols), BF16),
        input_output_aliases={2: 0} if held else {},
        cost_estimate=pl.CostEstimate(
            flops=2 * vectors * count * RI * n * cols,
            bytes_accessed=vectors * count * RI * (n + cols) * 2,
            transcendentals=0,
        ),
        compiler_params=grant(56),
        name="half",
    )(trial, chol, *([some] if held else []))


def taylor_kernel(*refs, counts):
    g_refs = refs[: len(counts)]
    q0_ref, half_ref, new_ref, send_ref, kept_ref, total, even, odd, sem = refs[len(counts) :]
    keep = pltpu.make_async_copy(half_ref.at[pl.ds(0, kept_ref.shape[0])], kept_ref, sem)
    keep.start()
    n, cols = q0_ref.shape
    nocc = cols // 2
    owners = g_refs[0].shape[0]
    rows = n // owners
    total[...] = q0_ref[...].astype(F32).reshape(owners, rows, cols)
    source = q0_ref
    for order in range(1, TAYLOR + 1):
        target = (even, odd)[order % 2]
        q = source[...].reshape(n, cols)
        start = 0
        for g_ref, count in zip(g_refs, counts):
            size = count * RI
            p = jnp.dot(g_ref[...].reshape(owners * size, n), q, preferred_element_type=F32)
            p = p.reshape(owners, size, cols) * (1.0 / order)
            term = jnp.concatenate([-p[:, :, nocc:], p[:, :, :nocc]], axis=2)
            total[:, start : start + size] += term
            if order < TAYLOR:
                target[:, start : start + size] = term.astype(BF16)
            start += size
        source = target
    fresh = total[...].astype(BF16)
    new_ref[...] = fresh.reshape(n, cols)
    for b in range(rows // RI):
        send_ref[:, :, b * cols : (b + 1) * cols] = fresh[:, b * RI : (b + 1) * RI]
    keep.wait()


def taylor(parts, counts, orbitals, halves):
    kept = (halves.shape[0] // 2,) + halves.shape[1:]
    n, cols = orbitals.shape
    owners = parts[0].shape[0]
    rows = n // owners
    return pl.pallas_call(
        functools.partial(taylor_kernel, counts=counts),
        in_specs=[VMEM] * (len(parts) + 1) + [HBM],
        out_specs=[VMEM] * 3,
        out_shape=[
            jax.ShapeDtypeStruct((n, cols), BF16),
            jax.ShapeDtypeStruct((owners, RI, rows // RI * cols), BF16),
            jax.ShapeDtypeStruct(kept, BF16),
        ],
        scratch_shapes=[
            pltpu.VMEM((owners, rows, cols), F32),
            pltpu.VMEM((owners, rows, cols), BF16),
            pltpu.VMEM((owners, rows, cols), BF16),
            pltpu.SemaphoreType.DMA,
        ],
        cost_estimate=pl.CostEstimate(flops=2 * TAYLOR * n * n * cols, bytes_accessed=n * (n + 3 * cols) * 2, transcendentals=0),
        compiler_params=grant(36),
        name="taylor",
    )(*parts, orbitals, halves)


def bias_kernel(*refs, cols):
    n_ref, k_ref, h_ref, o_ref, pair, rest, sems = refs
    w, _, depth = n_ref.shape
    vectors = h_ref.shape[0]
    wb = min(w, WB)
    nocc = cols // 2
    size = 128
    lanes = wb * 2 * RI
    sub = lax.broadcasted_iota(jnp.int32, (RI, lanes), 0)
    keep = lax.broadcasted_iota(jnp.int32, (RI, lanes), 1) % RI == sub
    kept = k_ref.shape[0]
    dmas = [
        pltpu.make_async_copy(h_ref.at[pl.ds(kept + v, size)], rest.at[pl.ds(v, size)], sems.at[v // size])
        for v in range(0, vectors - kept, size)
    ]
    for dma in dmas:
        dma.start()

    def block(k, fetched):
        for s in range(0, depth, cols):
            real = n_ref[pl.ds(k * wb, wb), :, s : s + cols].astype(F32)
            imag = jnp.concatenate([real[:, :, nocc:], -real[:, :, :nocc]], axis=2)
            pair[s : s + cols, :] = jnp.stack([real, imag], axis=1).reshape(lanes, cols).T.astype(BF16)
        for v in range(0, vectors, size):
            if v >= kept and not fetched:
                dmas[(v - kept) // size].wait()
            h = (k_ref[v : v + size] if v < kept else rest[v - kept : v - kept + size]).reshape(size * RI, depth)
            out = jnp.dot(h, pair[...], preferred_element_type=F32)
            out = jnp.where(keep[None], out.reshape(size, RI, lanes), 0.0).sum(axis=1)
            o_ref[pl.ds(k * wb, wb), :, v : v + size] = (
                out.T.reshape(wb * 2, RI, size).sum(axis=1).reshape(wb, 2, size)
            )

    block(0, False)
    if w > wb:
        pl.loop(1, w // wb)(lambda k: block(k, True))


def bias(rows, kept, halves, cols):
    w, _, depth = rows.shape
    vectors = halves.shape[0]
    wb = min(w, WB)
    return pl.pallas_call(
        functools.partial(bias_kernel, cols=cols),
        in_specs=[VMEM, VMEM, HBM],
        out_specs=VMEM,
        out_shape=jax.ShapeDtypeStruct((w, 2, vectors), F32),
        scratch_shapes=[
            pltpu.VMEM((depth, wb * 2 * RI), BF16),
            pltpu.VMEM((vectors - kept.shape[0],) + halves.shape[1:], BF16),
            pltpu.SemaphoreType.DMA(((vectors - kept.shape[0]) // 128,)),
        ],
        cost_estimate=pl.CostEstimate(
            flops=2 * vectors * RI * depth * w * 2 * RI, bytes_accessed=vectors * RI * depth * 2, transcendentals=0
        ),
        compiler_params=grant(40),
        name="bias",
    )(rows, kept, halves)


def splits(groups):
    first = max(1, 3 * groups // 8)
    return (first, groups - first) if groups > first else (groups,)


def exchange(v):
    return lax.all_to_all(v, "wide", split_axis=0, concat_axis=0, tiled=True)


def per_device(fields, chol, orbitals, trial):
    owners = lax.axis_size("wide")
    groups = chol.shape[1] // RI
    cols = trial.shape[1]
    counts = splits(groups)
    start = counts[0]
    stop = start + (min(2, counts[1]) if len(counts) > 1 else 0)
    everyone = exchange(copies(fields, owners))
    spread = expand(everyone)
    parts = [exchange(gen(spread, chol, trial, 0, counts[0], 0)[0])]
    some = None
    if len(counts) > 1:
        more, some = gen(spread, chol, trial, start, counts[1], stop - start)
        parts.append(exchange(more))
    halves = half(trial, chol, some, (start, stop))
    fresh, send, kept = taylor(parts, counts, orbitals[0], halves)
    rows_all = exchange(send)
    mine = exchange(bias(rows_all, kept, halves, cols))
    return fresh[None], mine.sum(axis=0, keepdims=True)


def solution(mesh):
    in_specs = (
        P(("groups", "wide"), None),
        P(None, "wide", None),
        P(("groups", "wide"), None, None),
        P(),
    )
    out_specs = (P(("groups", "wide"), None, None), P(("groups", "wide"), None, None))
    return jax.shard_map(
        per_device, mesh=mesh, in_specs=in_specs, out_specs=out_specs, check_vma=False
    )
```

```python
import functools

import jax
import jax.numpy as jnp
from jax import lax
from jax.experimental import pallas as pl
from jax.experimental.pallas import tpu as pltpu
from jax.sharding import PartitionSpec as P

TAYLOR = 4
RI = 8
WB = 16
BF16 = jnp.bfloat16
F32 = jnp.float32
MIB = 1 << 20
VMEM = pl.BlockSpec(memory_space=pltpu.VMEM)
HBM = pl.BlockSpec(memory_space=pltpu.HBM)


def grant(mib):
    return pltpu.CompilerParams(vmem_limit_bytes=mib * MIB)


def copies(fields, owners):
    def kernel(f_ref, o_ref):
        o_ref[...] = jnp.broadcast_to(f_ref[...].astype(F32)[:, None, :], o_ref.shape).astype(BF16)

    return pl.pallas_call(
        kernel,
        in_specs=[VMEM],
        out_specs=VMEM,
        out_shape=jax.ShapeDtypeStruct((owners, RI, fields.shape[1]), BF16),
        compiler_params=grant(4),
        name="copies",
    )(fields)


def expand(f):
    w, _, g = f.shape

    def kernel(f_ref, o_ref):
        fields = f_ref[...].astype(F32)[:, 0, :].astype(BF16)
        lane = lax.broadcasted_iota(jnp.int32, (128, 128 * RI), 1)
        row = lax.broadcasted_iota(jnp.int32, (128, 128 * RI), 0)
        repeat = (lane // RI == row).astype(F32).astype(BF16)
        sub = lax.broadcasted_iota(jnp.int32, (RI, 128 * RI), 0)
        keep = lax.broadcasted_iota(jnp.int32, (RI, 128 * RI), 1) % RI == sub
        for b in range(g // 128):
            v = jnp.dot(fields[:, b * 128 : (b + 1) * 128], repeat, preferred_element_type=F32)
            e = jnp.where(keep[None], v[:, None, :], 0.0)
            o_ref[:, b * 128 * RI : (b + 1) * 128 * RI] = e.reshape(w * RI, 128 * RI).astype(BF16)

    return pl.pallas_call(
        kernel,
        in_specs=[VMEM],
        out_specs=VMEM,
        out_shape=jax.ShapeDtypeStruct((w * RI, g * RI), BF16),
        compiler_params=grant(16),
        cost_estimate=pl.CostEstimate(flops=2 * w * g * 128 * RI, bytes_accessed=w * g * RI * RI * 2, transcendentals=0),
        name="expand",
    )(f)


def gen(fk, chol, trial, first, count, both):
    vectors, _, n = chol.shape
    cols = trial.shape[1]
    w = fk.shape[0] // RI
    wb = min(w, WB)
    pieces = 8
    size = vectors // pieces
    slots = 2 * pieces if both else pieces

    def kernel(fk_ref, c_ref, *refs):
        if both:
            t_ref, o_ref, h_ref, held, done, acc, in_sems, out_sems, side, side_sems = refs
        else:
            o_ref, held, done, acc, in_sems, out_sems = refs

        def fetch(group, piece, slot):
            return pltpu.make_async_copy(
                c_ref.at[pl.ds(piece * size, size), pl.ds(pl.multiple_of((first + group) * RI, RI), RI), :],
                held.at[slot],
                in_sems.at[slot],
            )

        def put(group, slot):
            return pltpu.make_async_copy(
                done.at[slot], o_ref.at[:, pl.ds(pl.multiple_of(group * RI, RI), RI), :], out_sems.at[slot]
            )

        def put_side(group, slot):
            return pltpu.make_async_copy(
                side.at[slot],
                h_ref.at[:, :, pl.ds(pl.multiple_of((first + group) * cols, cols), cols)],
                side_sems.at[slot],
            )

        def base(group):
            return lax.rem(group, 2) * pieces if both else 0

        for p in range(pieces - 1):
            fetch(0, p, p).start()

        def body(group, with_side):
            here, there = base(group), base(group + 1)
            for p in range(pieces):
                fetch(group, p, here + p).wait()
                if p == 0:
                    fetch(group, pieces - 1, here + pieces - 1).start()
                else:

                    @pl.when(group + 1 < count)
                    def _():
                        fetch(group + 1, p - 1, there + p - 1).start()

                x = held[here + p].reshape(size * RI, n)
                for k in range(w // wb):
                    r = slice(k * wb * RI, (k + 1) * wb * RI)
                    part = jnp.dot(fk_ref[r, p * size * RI : (p + 1) * size * RI], x, preferred_element_type=F32)
                    if p == 0:
                        acc[r] = part
                    else:
                        acc[r] += part
            if with_side:
                x = held[pl.ds(here, pieces)].reshape(vectors * RI, n)
                product = jnp.dot(x, t_ref[...], preferred_element_type=F32)
                side[group] = product.reshape(vectors, RI, cols).astype(BF16)
            slot = lax.rem(group, 2)

            @pl.when(group >= 2)
            def _():
                put(group - 2, slot).wait()

            done[slot] = acc[...].reshape(w, RI, n).astype(BF16)
            put(group, slot).start()
            if with_side:
                put_side(group, group).start()

        if both:
            pl.loop(0, both)(lambda group: body(group, True))
        if both < count:
            pl.loop(both, count)(lambda group: body(group, False))
        for group in range(max(0, count - 2), count):
            put(group, group % 2).wait()
        for group in range(both):
            put_side(group, group).wait()

    rows_out = jax.ShapeDtypeStruct((w, count * RI, n), BF16)
    half_out = jax.ShapeDtypeStruct((vectors, RI, chol.shape[1] // RI * cols), BF16)
    out = pl.pallas_call(
        kernel,
        in_specs=[VMEM, HBM] + [VMEM] * bool(both),
        out_specs=[HBM, HBM] if both else HBM,
        out_shape=[rows_out, half_out] if both else rows_out,
        scratch_shapes=[
            pltpu.VMEM((slots, size, RI, n), BF16),
            pltpu.VMEM((2, w, RI, n), BF16),
            pltpu.VMEM((w * RI, n), F32),
            pltpu.SemaphoreType.DMA((slots,)),
            pltpu.SemaphoreType.DMA((2,)),
        ]
        + ([pltpu.VMEM((both, vectors, RI, cols), BF16), pltpu.SemaphoreType.DMA((both,))] if both else []),
        cost_estimate=pl.CostEstimate(
            flops=2 * w * RI * vectors * count * RI * n, bytes_accessed=vectors * count * RI * n * 2, transcendentals=0
        ),
        compiler_params=grant(56 if both else 16 + w // 4),
    )(fk, chol, *([trial] if both else []))
    return out if both else (out, None)


def half(trial, chol, some, skip):
    vectors, rows, n = chol.shape
    cols = trial.shape[1]
    groups = rows // RI
    start, stop = skip
    count = groups - (stop - start)

    def kernel(t_ref, x_ref, *refs):
        o_ref = refs[-1]
        x = x_ref[...].reshape(vectors * RI, n)
        p = jnp.dot(x, t_ref[...], preferred_element_type=F32)
        o_ref[...] = p.reshape(o_ref.shape).astype(BF16)

    def group(i):
        return jnp.where(i < start, i, i + (stop - start))

    held = some is not None
    return pl.pallas_call(
        kernel,
        grid=(count,),
        in_specs=[
            pl.BlockSpec((n, cols), lambda i: (0, 0)),
            pl.BlockSpec((vectors, RI, n), lambda i: (0, group(i), 0)),
        ]
        + [HBM] * held,
        out_specs=pl.BlockSpec((vectors, RI, cols), lambda i: (0, 0, group(i))),
        out_shape=jax.ShapeDtypeStruct((vectors, RI, groups * cols), BF16),
        input_output_aliases={2: 0} if held else {},
        cost_estimate=pl.CostEstimate(
            flops=2 * vectors * count * RI * n * cols,
            bytes_accessed=vectors * count * RI * (n + cols) * 2,
            transcendentals=0,
        ),
        compiler_params=grant(56),
        name="half",
    )(trial, chol, *([some] if held else []))


def taylor_kernel(*refs, counts):
    g_refs = refs[: len(counts)]
    q0_ref, half_ref, new_ref, send_ref, kept_ref, total, even, odd, sem = refs[len(counts) :]
    keep = pltpu.make_async_copy(half_ref.at[pl.ds(0, kept_ref.shape[0])], kept_ref, sem)

    @pl.when(lax.axis_index("wide") >= 0)
    def _():
        keep.start()

    n, cols = q0_ref.shape
    nocc = cols // 2
    owners = g_refs[0].shape[0]
    rows = n // owners
    total[...] = q0_ref[...].astype(F32).reshape(owners, rows, cols)
    source = q0_ref
    for order in range(1, TAYLOR + 1):
        target = (even, odd)[order % 2]
        q = source[...].reshape(n, cols)
        start = 0
        for g_ref, count in zip(g_refs, counts):
            size = count * RI
            p = jnp.dot(g_ref[...].reshape(owners * size, n), q, preferred_element_type=F32)
            p = p.reshape(owners, size, cols) * (1.0 / order)
            term = jnp.concatenate([-p[:, :, nocc:], p[:, :, :nocc]], axis=2)
            total[:, start : start + size] += term
            if order < TAYLOR:
                target[:, start : start + size] = term.astype(BF16)
            start += size
        source = target
    fresh = total[...].astype(BF16)
    new_ref[...] = fresh.reshape(n, cols)
    for b in range(rows // RI):
        send_ref[:, :, b * cols : (b + 1) * cols] = fresh[:, b * RI : (b + 1) * RI]
    keep.wait()


def taylor(parts, counts, orbitals, halves):
    kept = (halves.shape[0] // 2,) + halves.shape[1:]
    n, cols = orbitals.shape
    owners = parts[0].shape[0]
    rows = n // owners
    return pl.pallas_call(
        functools.partial(taylor_kernel, counts=counts),
        in_specs=[VMEM] * (len(parts) + 1) + [HBM],
        out_specs=[VMEM] * 3,
        out_shape=[
            jax.ShapeDtypeStruct((n, cols), BF16),
            jax.ShapeDtypeStruct((owners, RI, rows // RI * cols), BF16),
            jax.ShapeDtypeStruct(kept, BF16),
        ],
        scratch_shapes=[
            pltpu.VMEM((owners, rows, cols), F32),
            pltpu.VMEM((owners, rows, cols), BF16),
            pltpu.VMEM((owners, rows, cols), BF16),
            pltpu.SemaphoreType.DMA,
        ],
        cost_estimate=pl.CostEstimate(flops=2 * TAYLOR * n * n * cols, bytes_accessed=n * (n + 3 * cols) * 2, transcendentals=0),
        compiler_params=grant(36),
        name="taylor",
    )(*parts, orbitals, halves)


def bias_kernel(*refs, cols):
    n_ref, k_ref, h_ref, o_ref, pair, rest, sems = refs
    w, _, depth = n_ref.shape
    vectors = h_ref.shape[0]
    wb = min(w, WB)
    nocc = cols // 2
    size = 128
    lanes = wb * 2 * RI
    sub = lax.broadcasted_iota(jnp.int32, (RI, lanes), 0)
    keep = lax.broadcasted_iota(jnp.int32, (RI, lanes), 1) % RI == sub
    kept = k_ref.shape[0]

    def fetch(piece):
        at = pl.ds(piece * size, size)
        return pltpu.make_async_copy(h_ref.at[pl.ds(kept + piece * size, size)], rest.at[at], sems.at[piece])

    pl.loop(0, (vectors - kept) // size)(lambda piece: fetch(piece).start())

    def block(k, fetched):
        for s in range(0, depth, cols):
            real = n_ref[pl.ds(k * wb, wb), :, s : s + cols].astype(F32)
            imag = jnp.concatenate([real[:, :, nocc:], -real[:, :, :nocc]], axis=2)
            pair[s : s + cols, :] = jnp.stack([real, imag], axis=1).reshape(lanes, cols).T.astype(BF16)

        def piece(h, v):
            out = jnp.dot(h.reshape(size * RI, depth), pair[...], preferred_element_type=F32)
            out = jnp.where(keep[None], out.reshape(size, RI, lanes), 0.0).sum(axis=1)
            o_ref[pl.ds(k * wb, wb), :, pl.ds(pl.multiple_of(v, size), size)] = (
                out.T.reshape(wb * 2, RI, size).sum(axis=1).reshape(wb, 2, size)
            )

        @pl.loop(0, kept // size)
        def _(i):
            piece(k_ref[pl.ds(i * size, size)], i * size)

        @pl.loop(0, (vectors - kept) // size)
        def _(i):
            if not fetched:
                fetch(i).wait()
            piece(rest[pl.ds(i * size, size)], kept + i * size)

    block(0, False)
    if w > wb:
        pl.loop(1, w // wb)(lambda k: block(k, True))


def bias(rows, kept, halves, cols):
    w, _, depth = rows.shape
    vectors = halves.shape[0]
    wb = min(w, WB)
    return pl.pallas_call(
        functools.partial(bias_kernel, cols=cols),
        in_specs=[VMEM, VMEM, HBM],
        out_specs=VMEM,
        out_shape=jax.ShapeDtypeStruct((w, 2, vectors), F32),
        scratch_shapes=[
            pltpu.VMEM((depth, wb * 2 * RI), BF16),
            pltpu.VMEM((vectors - kept.shape[0],) + halves.shape[1:], BF16),
            pltpu.SemaphoreType.DMA(((vectors - kept.shape[0]) // 128,)),
        ],
        cost_estimate=pl.CostEstimate(
            flops=2 * vectors * RI * depth * w * 2 * RI, bytes_accessed=vectors * RI * depth * 2, transcendentals=0
        ),
        compiler_params=grant(40),
        name="bias",
    )(rows, kept, halves)


def splits(groups):
    first = max(1, 3 * groups // 8)
    return (first, groups - first) if groups > first else (groups,)


def exchange(v):
    return lax.all_to_all(v, "wide", split_axis=0, concat_axis=0, tiled=True)


def per_device(fields, chol, orbitals, trial):
    owners = lax.axis_size("wide")
    groups = chol.shape[1] // RI
    cols = trial.shape[1]
    counts = splits(groups)
    start = counts[0]
    stop = start + (min(1, counts[1]) if len(counts) > 1 else 0)
    everyone = exchange(copies(fields, owners))
    spread = expand(everyone)
    parts = [exchange(gen(spread, chol, trial, 0, counts[0], 0)[0])]
    some = None
    if len(counts) > 1:
        more, some = gen(spread, chol, trial, start, counts[1], stop - start)
        parts.append(exchange(more))
    halves = half(trial, chol, some, (start, stop))
    fresh, send, kept = taylor(parts, counts, orbitals[0], halves)
    rows_all = exchange(send)
    mine = exchange(bias(rows_all, kept, halves, cols))
    return fresh[None], mine.sum(axis=0, keepdims=True)


def solution(mesh):
    in_specs = (
        P(("groups", "wide"), None),
        P(None, "wide", None),
        P(("groups", "wide"), None, None),
        P(),
    )
    out_specs = (P(("groups", "wide"), None, None), P(("groups", "wide"), None, None))
    return jax.shard_map(
        per_device, mesh=mesh, in_specs=in_specs, out_specs=out_specs, check_vma=False
    )
```

```python
import functools

import jax
import jax.numpy as jnp
from jax import lax
from jax.experimental import pallas as pl
from jax.experimental.pallas import tpu as pltpu
from jax.sharding import PartitionSpec as P

TAYLOR = 4
RI = 8
WB = 32
BF16 = jnp.bfloat16
F32 = jnp.float32
MIB = 1 << 20
VMEM = pl.BlockSpec(memory_space=pltpu.VMEM)
HBM = pl.BlockSpec(memory_space=pltpu.HBM)


def grant(mib):
    return pltpu.CompilerParams(vmem_limit_bytes=mib * MIB)


def copies(fields, owners):
    rows = fields.shape[1] // 128

    def kernel(f_ref, o_ref):
        f = f_ref[...].astype(F32)
        f = jnp.concatenate([f[:, b * 128 : (b + 1) * 128] for b in range(rows)], axis=0)
        o_ref[...] = jnp.broadcast_to(f[None], o_ref.shape).astype(BF16)

    return pl.pallas_call(
        kernel,
        in_specs=[VMEM],
        out_specs=VMEM,
        out_shape=jax.ShapeDtypeStruct((owners, rows, 128), BF16),
        compiler_params=grant(4),
        name="copies",
    )(fields)


def expand(f):
    w, g = f.shape[0], f.shape[1] * f.shape[2]

    def kernel(f_ref, o_ref):
        fields = f_ref[...].astype(F32)
        lane = lax.broadcasted_iota(jnp.int32, (128, 128 * RI), 1)
        row = lax.broadcasted_iota(jnp.int32, (128, 128 * RI), 0)
        repeat = (lane // RI == row).astype(F32).astype(BF16)
        sub = lax.broadcasted_iota(jnp.int32, (RI, 128 * RI), 0)
        keep = lax.broadcasted_iota(jnp.int32, (RI, 128 * RI), 1) % RI == sub
        for b in range(g // 128):
            v = jnp.dot(fields[:, b, :].astype(BF16), repeat, preferred_element_type=F32)
            e = jnp.where(keep[None], v[:, None, :], 0.0)
            o_ref[:, b * 128 * RI : (b + 1) * 128 * RI] = e.reshape(w * RI, 128 * RI).astype(BF16)

    return pl.pallas_call(
        kernel,
        in_specs=[VMEM],
        out_specs=VMEM,
        out_shape=jax.ShapeDtypeStruct((w * RI, g * RI), BF16),
        compiler_params=grant(16),
        cost_estimate=pl.CostEstimate(flops=2 * w * g * 128 * RI, bytes_accessed=w * g * RI * RI * 2, transcendentals=0),
        name="expand",
    )(f)


def gen(fk, chol, share, first, count):
    vectors, rows, n = chol.shape
    w = fk.shape[0] // RI
    wb = min(w, WB)
    pieces = 8
    size = vectors // pieces
    slots = 2 * pieces
    ahead = 4

    def kernel(fk_ref, c_ref, o_ref, held, done, acc, in_sems, out_sems):
        base = first + share.first_group(rows)

        def fetch(group, piece):
            slot = lax.rem(group, 2) * pieces + piece
            return pltpu.make_async_copy(
                c_ref.at[pl.ds(piece * size, size), pl.ds(pl.multiple_of((base + group) * RI, RI), RI), :],
                held.at[slot],
                in_sems.at[slot],
            )

        def put(group, slot):
            return pltpu.make_async_copy(
                done.at[slot], o_ref.at[:, pl.ds(pl.multiple_of(group * RI, RI), RI), :], out_sems.at[slot]
            )

        for p in range(min(ahead, count * pieces)):
            fetch(p // pieces, p % pieces).start()

        @pl.loop(0, count)
        def _(group):
            for p in range(pieces):
                fetch(group, p).wait()
                later, piece = divmod(p + ahead, pieces)

                @pl.when(group + later < count)
                def _():
                    fetch(group + later, piece).start()

                x = held[lax.rem(group, 2) * pieces + p].reshape(size * RI, n)
                for k in range(w // wb):
                    r = slice(k * wb * RI, (k + 1) * wb * RI)
                    part = jnp.dot(fk_ref[r, p * size * RI : (p + 1) * size * RI], x, preferred_element_type=F32)
                    if p == 0:
                        acc[r] = part
                    else:
                        acc[r] += part
            slot = lax.rem(group, 2)

            @pl.when(group >= 2)
            def _():
                put(group - 2, slot).wait()

            done[slot] = acc[...].reshape(w, RI, n).astype(BF16)
            put(group, slot).start()

        for group in range(max(0, count - 2), count):
            put(group, group % 2).wait()

    return pl.pallas_call(
        kernel,
        in_specs=[VMEM, HBM],
        out_specs=HBM,
        out_shape=jax.ShapeDtypeStruct((w, count * RI, n), BF16),
        scratch_shapes=[
            pltpu.VMEM((slots, size, RI, n), BF16),
            pltpu.VMEM((2, w, RI, n), BF16),
            pltpu.VMEM((w * RI, n), F32),
            pltpu.SemaphoreType.DMA((slots,)),
            pltpu.SemaphoreType.DMA((2,)),
        ],
        cost_estimate=pl.CostEstimate(
            flops=2 * w * RI * vectors * count * RI * n, bytes_accessed=vectors * count * RI * n * 2, transcendentals=0
        ),
        compiler_params=grant(56 if first else 24 + w // 8),
    )(fk, chol)


def half(trial, chol):
    vectors, rows, n = chol.shape
    cols = trial.shape[1]
    count = rows // RI

    def kernel(t_ref, x_ref, o_ref):
        x = x_ref[...].reshape(vectors * RI, n)
        p = jnp.dot(x, t_ref[...], preferred_element_type=F32)
        o_ref[...] = p.reshape(o_ref.shape).astype(BF16)

    return pl.pallas_call(
        kernel,
        grid=(count,),
        in_specs=[
            pl.BlockSpec((n, cols), lambda i: (0, 0)),
            pl.BlockSpec((vectors, RI, n), lambda i: (0, i, 0)),
        ],
        out_specs=pl.BlockSpec((vectors, RI, cols), lambda i: (0, 0, i)),
        out_shape=jax.ShapeDtypeStruct((vectors, RI, count * cols), BF16),
        cost_estimate=pl.CostEstimate(
            flops=2 * vectors * count * RI * n * cols,
            bytes_accessed=vectors * count * RI * (n + cols) * 2,
            transcendentals=0,
        ),
        compiler_params=grant(56),
        name="half",
    )(trial, chol)


def taylor_kernel(*refs, counts, parts):
    g_refs = refs[: len(counts)]
    q0_ref, half_ref, new_ref, send_ref, kept_ref, total, even, odd, sems = refs[len(counts) :]
    piece = kept_ref.shape[0] // sems.shape[0]

    def keep(i):
        at = pl.ds(i * piece, piece)
        return pltpu.make_async_copy(half_ref.at[at], kept_ref.at[at], sems.at[i])

    pl.loop(0, sems.shape[0])(lambda i: keep(i).start())
    n, cols = q0_ref.shape
    nocc = cols // 2
    senders = g_refs[0].shape[0]
    owners = senders // parts
    rows = n // owners
    total[...] = q0_ref[...].astype(F32).reshape(owners, rows, cols)
    source = q0_ref
    for order in range(1, TAYLOR + 1):
        target = (even, odd)[order % 2]
        q = source[...].reshape(n, cols)
        start = 0
        for g_ref, count in zip(g_refs, counts):
            size = count * RI
            p = jnp.dot(g_ref[...].reshape(senders * size, n), q, preferred_element_type=F32)
            p = p.reshape(senders, size, cols) * (1.0 / order)
            term = jnp.concatenate([-p[:, :, nocc:], p[:, :, :nocc]], axis=2)
            for part in range(parts):
                mine = term[part * owners : (part + 1) * owners]
                at = part * (rows // parts) + start
                total[:, at : at + size] += mine
                if order < TAYLOR:
                    target[:, at : at + size] = mine.astype(BF16)
            start += size
        source = target
    fresh = total[...].astype(BF16)
    new_ref[...] = fresh.reshape(n, cols)
    for b in range(rows // RI):
        send_ref[:, :, b * cols : (b + 1) * cols] = fresh[:, b * RI : (b + 1) * RI]
    pl.loop(0, sems.shape[0])(lambda i: keep(i).wait())


def taylor(received, counts, parts, orbitals, halves):
    kept = (halves.shape[0] // 2,) + halves.shape[1:]
    n, cols = orbitals.shape
    senders = received[0].shape[0]
    owners = senders // parts
    rows = n // owners
    return pl.pallas_call(
        functools.partial(taylor_kernel, counts=counts, parts=parts),
        in_specs=[VMEM] * (len(received) + 1) + [HBM],
        out_specs=[VMEM] * 3,
        out_shape=[
            jax.ShapeDtypeStruct((n, cols), BF16),
            jax.ShapeDtypeStruct((owners, RI, rows // RI * cols), BF16),
            jax.ShapeDtypeStruct(kept, BF16),
        ],
        scratch_shapes=[
            pltpu.VMEM((owners, rows, cols), F32),
            pltpu.VMEM((owners, rows, cols), BF16),
            pltpu.VMEM((owners, rows, cols), BF16),
            pltpu.SemaphoreType.DMA((8,)),
        ],
        cost_estimate=pl.CostEstimate(flops=2 * TAYLOR * n * n * cols, bytes_accessed=n * (n + 3 * cols) * 2, transcendentals=0),
        compiler_params=grant(36),
        name="taylor",
    )(*received, orbitals, halves)


def bias_kernel(*refs, cols):
    n_ref, k_ref, h_ref, o_ref, pair, rest, sems = refs
    w, _, depth = n_ref.shape
    vectors = h_ref.shape[0]
    wb = min(w, WB)
    nocc = cols // 2
    size = 128
    lanes = wb * 2 * RI
    sub = lax.broadcasted_iota(jnp.int32, (RI, lanes), 0)
    keep = lax.broadcasted_iota(jnp.int32, (RI, lanes), 1) % RI == sub
    kept = k_ref.shape[0]

    def fetch(piece):
        at = pl.ds(piece * size, size)
        return pltpu.make_async_copy(h_ref.at[pl.ds(kept + piece * size, size)], rest.at[at], sems.at[piece])

    pl.loop(0, (vectors - kept) // size)(lambda piece: fetch(piece).start())

    def block(k, fetched):
        for s in range(0, depth, cols):
            real = n_ref[pl.ds(k * wb, wb), :, s : s + cols].astype(F32)
            imag = jnp.concatenate([real[:, :, nocc:], -real[:, :, :nocc]], axis=2)
            pair[s : s + cols, :] = jnp.stack([real, imag], axis=1).reshape(lanes, cols).T.astype(BF16)

        def piece(h, v):
            out = jnp.dot(h.reshape(size * RI, depth), pair[...], preferred_element_type=F32)
            out = jnp.where(keep[None], out.reshape(size, RI, lanes), 0.0).sum(axis=1)
            o_ref[pl.ds(k * wb, wb), :, pl.ds(pl.multiple_of(v, size), size)] = (
                out.T.reshape(wb * 2, RI, size).sum(axis=1).reshape(wb, 2, size)
            )

        @pl.loop(0, kept // size)
        def _(i):
            piece(k_ref[pl.ds(i * size, size)], i * size)

        @pl.loop(0, (vectors - kept) // size)
        def _(i):
            if not fetched:
                fetch(i).wait()
            piece(rest[pl.ds(i * size, size)], kept + i * size)

    block(0, False)
    if w > wb:
        pl.loop(1, w // wb)(lambda k: block(k, True))


def bias(rows, kept, halves, cols):
    w, _, depth = rows.shape
    vectors = halves.shape[0]
    wb = min(w, WB)
    return pl.pallas_call(
        functools.partial(bias_kernel, cols=cols),
        in_specs=[VMEM, VMEM, HBM],
        out_specs=VMEM,
        out_shape=jax.ShapeDtypeStruct((w, 2, vectors), F32),
        scratch_shapes=[
            pltpu.VMEM((depth, wb * 2 * RI), BF16),
            pltpu.VMEM((vectors - kept.shape[0],) + halves.shape[1:], BF16),
            pltpu.SemaphoreType.DMA(((vectors - kept.shape[0]) // 128,)),
        ],
        cost_estimate=pl.CostEstimate(
            flops=2 * vectors * RI * depth * w * 2 * RI, bytes_accessed=vectors * RI * depth * 2, transcendentals=0
        ),
        compiler_params=grant(40),
        name="bias",
    )(rows, kept, halves)


class Share:
    def __init__(self, rows):
        holders = lax.axis_size("groups")
        self.parts = holders if rows // RI % holders == 0 else 1
        self.axes = ("groups", "wide") if self.parts > 1 else "wide"
        self.senders = self.parts * lax.axis_size("wide")

    def first_group(self, rows):
        return lax.axis_index("groups") * (rows // RI // self.parts) if self.parts > 1 else 0


def exchange(v, axes):
    return lax.all_to_all(v, axes, split_axis=0, concat_axis=0, tiled=True)


def splits(groups):
    first = max(1, groups // 4)
    return (first, groups - first) if groups > first else (groups,)


def per_device(fields, chol, orbitals, trial):
    rows = chol.shape[1]
    share = Share(rows)
    counts = splits(rows // RI // share.parts)
    everyone = exchange(copies(fields, share.senders), share.axes)
    spread = expand(everyone)
    received = []
    start = 0
    for count in counts:
        made = gen(spread, chol, share, start, count)
        received.append(exchange(made, share.axes))
        start += count
    halves = half(trial, chol)
    fresh, send, kept = taylor(received, counts, share.parts, orbitals[0], halves)
    rows_all = exchange(send, "wide")
    mine = exchange(bias(rows_all, kept, halves, trial.shape[1]), "wide")
    return fresh[None], mine.sum(axis=0, keepdims=True)


def solution(mesh):
    in_specs = (
        P(("groups", "wide"), None),
        P(None, "wide", None),
        P(("groups", "wide"), None, None),
        P(),
    )
    out_specs = (P(("groups", "wide"), None, None), P(("groups", "wide"), None, None))
    return jax.shard_map(
        per_device, mesh=mesh, in_specs=in_specs, out_specs=out_specs, check_vma=False
    )
```

```python
import functools

import jax
import jax.numpy as jnp
from jax import lax
from jax.experimental import pallas as pl
from jax.experimental.pallas import tpu as pltpu
from jax.sharding import PartitionSpec as P

TAYLOR = 4
RI = 8
WB = 32
BF16 = jnp.bfloat16
F32 = jnp.float32
MIB = 1 << 20
VMEM = pl.BlockSpec(memory_space=pltpu.VMEM)
HBM = pl.BlockSpec(memory_space=pltpu.HBM)


def grant(mib):
    return pltpu.CompilerParams(vmem_limit_bytes=mib * MIB)


def copies(fields, owners):
    rows = fields.shape[1] // 128

    def kernel(f_ref, o_ref):
        f = f_ref[...].astype(F32)
        f = jnp.concatenate([f[:, b * 128 : (b + 1) * 128] for b in range(rows)], axis=0)
        o_ref[...] = jnp.broadcast_to(f[None], o_ref.shape).astype(BF16)

    return pl.pallas_call(
        kernel,
        in_specs=[VMEM],
        out_specs=VMEM,
        out_shape=jax.ShapeDtypeStruct((owners, rows, 128), BF16),
        compiler_params=grant(4),
        name="copies",
    )(fields)


def spread_fields(f_ref, o_ref):
    w, blocks, width = f_ref.shape
    fields = f_ref[...].astype(F32)
    lane = lax.broadcasted_iota(jnp.int32, (width, width * RI), 1)
    row = lax.broadcasted_iota(jnp.int32, (width, width * RI), 0)
    repeat = (lane // RI == row).astype(F32).astype(BF16)
    sub = lax.broadcasted_iota(jnp.int32, (RI, width * RI), 0)
    keep = lax.broadcasted_iota(jnp.int32, (RI, width * RI), 1) % RI == sub
    for b in range(blocks):
        v = jnp.dot(fields[:, b, :].astype(BF16), repeat, preferred_element_type=F32)
        e = jnp.where(keep[None], v[:, None, :], 0.0)
        o_ref[:, b * width * RI : (b + 1) * width * RI] = e.reshape(w * RI, width * RI).astype(BF16)


def gen(source, chol, share, first, count):
    vectors, rows, n = chol.shape
    fresh = source.ndim == 3
    w = source.shape[0] if fresh else source.shape[0] // RI
    wb = min(w, WB)
    pieces, ahead = 8, 8
    size = vectors // pieces
    slots = 2 * pieces

    def kernel(s_ref, c_ref, *refs):
        if fresh:
            o_ref, spread_ref, *refs = refs
        else:
            o_ref, *refs = refs
        fk_ref, held, done, acc, in_sems, out_sems, spread_sem = refs
        base = first + share.first_group(rows)

        def fetch(group, piece):
            slot = lax.rem(group, 2) * pieces + piece
            return pltpu.make_async_copy(
                c_ref.at[pl.ds(piece * size, size), pl.ds(pl.multiple_of((base + group) * RI, RI), RI), :],
                held.at[slot],
                in_sems.at[slot],
            )

        def put(group, slot):
            return pltpu.make_async_copy(
                done.at[slot], o_ref.at[:, pl.ds(pl.multiple_of(group * RI, RI), RI), :], out_sems.at[slot]
            )

        if not fresh:
            spread = pltpu.make_async_copy(s_ref, fk_ref, spread_sem)
            spread.start()

        @pl.loop(0, min(ahead, count * pieces))
        def _(p):
            fetch(p // pieces, lax.rem(p, pieces)).start()

        if fresh:
            spread_fields(s_ref, fk_ref)
            spread = pltpu.make_async_copy(fk_ref, spread_ref, spread_sem)
            spread.start()
        else:
            spread.wait()

        @pl.loop(0, count)
        def _(group):
            for p in range(pieces):
                fetch(group, p).wait()
                later, piece = divmod(p + ahead, pieces)

                @pl.when(group + later < count)
                def _():
                    fetch(group + later, piece).start()

                x = held[lax.rem(group, 2) * pieces + p].reshape(size * RI, n)
                for k in range(w // wb):
                    r = slice(k * wb * RI, (k + 1) * wb * RI)
                    part = jnp.dot(fk_ref[r, p * size * RI : (p + 1) * size * RI], x, preferred_element_type=F32)
                    if p == 0:
                        acc[r] = part
                    else:
                        acc[r] += part
            slot = lax.rem(group, 2)

            @pl.when(group >= 2)
            def _():
                put(group - 2, slot).wait()

            done[slot] = acc[...].reshape(w, RI, n).astype(BF16)
            put(group, slot).start()

        for group in range(max(0, count - 2), count):
            put(group, group % 2).wait()
        if fresh:
            spread.wait()

    rows_out = jax.ShapeDtypeStruct((w, count * RI, n), BF16)
    spread_out = jax.ShapeDtypeStruct((w * RI, vectors * RI), BF16)
    out = pl.pallas_call(
        kernel,
        in_specs=[VMEM if fresh else HBM, HBM],
        out_specs=[HBM, HBM] if fresh else HBM,
        out_shape=[rows_out, spread_out] if fresh else rows_out,
        scratch_shapes=[
            pltpu.VMEM((w * RI, vectors * RI), BF16),
            pltpu.VMEM((slots, size, RI, n), BF16),
            pltpu.VMEM((2, w, RI, n), BF16),
            pltpu.VMEM((w * RI, n), F32),
            pltpu.SemaphoreType.DMA((slots,)),
            pltpu.SemaphoreType.DMA((2,)),
            pltpu.SemaphoreType.DMA,
        ],
        cost_estimate=pl.CostEstimate(
            flops=2 * w * RI * vectors * count * RI * n, bytes_accessed=vectors * count * RI * n * 2, transcendentals=0
        ),
        compiler_params=grant(58),
    )(source, chol)
    return out if fresh else (out, source)


def half(trial, chol):
    vectors, rows, n = chol.shape
    cols = trial.shape[1]
    count = rows // RI

    def kernel(t_ref, x_ref, o_ref):
        x = x_ref[...].reshape(vectors * RI, n)
        p = jnp.dot(x, t_ref[...], preferred_element_type=F32)
        o_ref[...] = p.reshape(o_ref.shape).astype(BF16)

    return pl.pallas_call(
        kernel,
        grid=(count,),
        in_specs=[
            pl.BlockSpec((n, cols), lambda i: (0, 0)),
            pl.BlockSpec((vectors, RI, n), lambda i: (0, i, 0)),
        ],
        out_specs=pl.BlockSpec((vectors, RI, cols), lambda i: (0, 0, i)),
        out_shape=jax.ShapeDtypeStruct((vectors, RI, count * cols), BF16),
        cost_estimate=pl.CostEstimate(
            flops=2 * vectors * count * RI * n * cols,
            bytes_accessed=vectors * count * RI * (n + cols) * 2,
            transcendentals=0,
        ),
        compiler_params=grant(56),
        name="half",
    )(trial, chol)


def taylor_kernel(*refs, counts, parts):
    g_refs = refs[: len(counts)]
    q0_ref, half_ref, new_ref, send_ref, kept_ref, total, even, odd, sems = refs[len(counts) :]
    piece = kept_ref.shape[0] // sems.shape[0]

    def keep(i):
        at = pl.ds(i * piece, piece)
        return pltpu.make_async_copy(half_ref.at[at], kept_ref.at[at], sems.at[i])

    pl.loop(0, sems.shape[0])(lambda i: keep(i).start())
    n, cols = q0_ref.shape
    nocc = cols // 2
    senders = g_refs[0].shape[0]
    owners = senders // parts
    rows = n // owners
    total[...] = q0_ref[...].astype(F32).reshape(owners, rows, cols)
    source = q0_ref
    for order in range(1, TAYLOR + 1):
        target = (even, odd)[order % 2]
        q = source[...].reshape(n, cols)
        start = 0
        for g_ref, count in zip(g_refs, counts):
            size = count * RI
            for part in range(parts):
                g = g_ref[part * owners : (part + 1) * owners].reshape(owners * size, n)
                p = jnp.dot(g, q, preferred_element_type=F32).reshape(owners, size, cols)
                if order > 1:
                    p = p * (1.0 / order)
                term = jnp.concatenate([-p[:, :, nocc:], p[:, :, :nocc]], axis=2)
                at = part * (rows // parts) + start
                total[:, at : at + size] += term
                if order < TAYLOR:
                    target[:, at : at + size] = term.astype(BF16)
            start += size
        source = target
    fresh = total[...].astype(BF16)
    new_ref[...] = fresh.reshape(n, cols)
    for b in range(rows // RI):
        send_ref[:, :, b * cols : (b + 1) * cols] = fresh[:, b * RI : (b + 1) * RI]
    pl.loop(0, sems.shape[0])(lambda i: keep(i).wait())


def taylor(received, counts, parts, orbitals, halves):
    kept = (halves.shape[0] // 2,) + halves.shape[1:]
    n, cols = orbitals.shape
    senders = received[0].shape[0]
    owners = senders // parts
    rows = n // owners
    return pl.pallas_call(
        functools.partial(taylor_kernel, counts=counts, parts=parts),
        in_specs=[VMEM] * (len(received) + 1) + [HBM],
        out_specs=[VMEM] * 3,
        out_shape=[
            jax.ShapeDtypeStruct((n, cols), BF16),
            jax.ShapeDtypeStruct((owners, RI, rows // RI * cols), BF16),
            jax.ShapeDtypeStruct(kept, BF16),
        ],
        scratch_shapes=[
            pltpu.VMEM((owners, rows, cols), F32),
            pltpu.VMEM((owners, rows, cols), BF16),
            pltpu.VMEM((owners, rows, cols), BF16),
            pltpu.SemaphoreType.DMA((8,)),
        ],
        cost_estimate=pl.CostEstimate(flops=2 * TAYLOR * n * n * cols, bytes_accessed=n * (n + 3 * cols) * 2, transcendentals=0),
        compiler_params=grant(36),
        name="taylor",
    )(*received, orbitals, halves)


def bias_kernel(*refs, cols):
    n_ref, k_ref, h_ref, o_ref, pair, rest, sems = refs
    w, _, depth = n_ref.shape
    vectors = h_ref.shape[0]
    wb = min(w, WB)
    nocc = cols // 2
    size = 128
    lanes = wb * 2 * RI
    sub = lax.broadcasted_iota(jnp.int32, (RI, lanes), 0)
    keep = lax.broadcasted_iota(jnp.int32, (RI, lanes), 1) % RI == sub
    kept = k_ref.shape[0]

    def fetch(piece):
        at = pl.ds(piece * size, size)
        return pltpu.make_async_copy(h_ref.at[pl.ds(kept + piece * size, size)], rest.at[at], sems.at[piece])

    pl.loop(0, (vectors - kept) // size)(lambda piece: fetch(piece).start())

    def block(k, fetched):
        for s in range(0, depth, cols):
            real = n_ref[pl.ds(k * wb, wb), :, s : s + cols].astype(F32)
            imag = jnp.concatenate([real[:, :, nocc:], -real[:, :, :nocc]], axis=2)
            pair[s : s + cols, :] = jnp.stack([real, imag], axis=1).reshape(lanes, cols).T.astype(BF16)

        def piece(h, v):
            out = jnp.dot(h.reshape(size * RI, depth), pair[...], preferred_element_type=F32)
            out = jnp.where(keep[None], out.reshape(size, RI, lanes), 0.0).sum(axis=1)
            o_ref[pl.ds(k * wb, wb), :, pl.ds(pl.multiple_of(v, size), size)] = (
                out.T.reshape(wb * 2, RI, size).sum(axis=1).reshape(wb, 2, size)
            )

        @pl.loop(0, kept // size)
        def _(i):
            piece(k_ref[pl.ds(i * size, size)], i * size)

        @pl.loop(0, (vectors - kept) // size)
        def _(i):
            if not fetched:
                fetch(i).wait()
            piece(rest[pl.ds(i * size, size)], kept + i * size)

    block(0, False)
    if w > wb:
        pl.loop(1, w // wb)(lambda k: block(k, True))


def bias(rows, kept, halves, cols):
    w, _, depth = rows.shape
    vectors = halves.shape[0]
    wb = min(w, WB)
    return pl.pallas_call(
        functools.partial(bias_kernel, cols=cols),
        in_specs=[VMEM, VMEM, HBM],
        out_specs=VMEM,
        out_shape=jax.ShapeDtypeStruct((w, 2, vectors), F32),
        scratch_shapes=[
            pltpu.VMEM((depth, wb * 2 * RI), BF16),
            pltpu.VMEM((vectors - kept.shape[0],) + halves.shape[1:], BF16),
            pltpu.SemaphoreType.DMA(((vectors - kept.shape[0]) // 128,)),
        ],
        cost_estimate=pl.CostEstimate(
            flops=2 * vectors * RI * depth * w * 2 * RI, bytes_accessed=vectors * RI * depth * 2, transcendentals=0
        ),
        compiler_params=grant(40),
        name="bias",
    )(rows, kept, halves)


class Share:
    def __init__(self, rows):
        holders = lax.axis_size("groups")
        self.parts = holders if rows // RI % holders == 0 else 1
        self.axes = ("groups", "wide") if self.parts > 1 else "wide"
        self.senders = self.parts * lax.axis_size("wide")

    def first_group(self, rows):
        return lax.axis_index("groups") * (rows // RI // self.parts) if self.parts > 1 else 0


def exchange(v, axes):
    return lax.all_to_all(v, axes, split_axis=0, concat_axis=0, tiled=True)


def splits(groups):
    first = max(1, groups // 4)
    return (first, groups - first) if groups > first else (groups,)


def per_device(fields, chol, orbitals, trial):
    rows = chol.shape[1]
    share = Share(rows)
    counts = splits(rows // RI // share.parts)
    everyone = exchange(copies(fields, share.senders), share.axes)
    source = everyone
    received = []
    start = 0
    for count in counts:
        made, source = gen(source, chol, share, start, count)
        received.append(exchange(made, share.axes))
        start += count
    halves = half(trial, chol)
    fresh, send, kept = taylor(received, counts, share.parts, orbitals[0], halves)
    rows_all = exchange(send, "wide")
    mine = exchange(bias(rows_all, kept, halves, trial.shape[1]), "wide")
    return fresh[None], mine.sum(axis=0, keepdims=True)


def solution(mesh):
    in_specs = (
        P(("groups", "wide"), None),
        P(None, "wide", None),
        P(("groups", "wide"), None, None),
        P(),
    )
    out_specs = (P(("groups", "wide"), None, None), P(("groups", "wide"), None, None))
    return jax.shard_map(
        per_device, mesh=mesh, in_specs=in_specs, out_specs=out_specs, check_vma=False
    )
```

```python
import functools

import jax
import jax.numpy as jnp
from jax import lax
from jax.experimental import pallas as pl
from jax.experimental.pallas import tpu as pltpu
from jax.sharding import PartitionSpec as P

TAYLOR = 4
RI = 8
WB = 16
BF16 = jnp.bfloat16
F32 = jnp.float32
MIB = 1 << 20
VMEM = pl.BlockSpec(memory_space=pltpu.VMEM)
HBM = pl.BlockSpec(memory_space=pltpu.HBM)


def grant(mib):
    return pltpu.CompilerParams(vmem_limit_bytes=mib * MIB)


def copies(fields, owners):
    rows = fields.shape[1] // 128

    def kernel(f_ref, o_ref):
        f = f_ref[...].astype(F32)
        f = jnp.concatenate([f[:, b * 128 : (b + 1) * 128] for b in range(rows)], axis=0)
        o_ref[...] = jnp.broadcast_to(f[None], o_ref.shape).astype(BF16)

    return pl.pallas_call(
        kernel,
        in_specs=[VMEM],
        out_specs=VMEM,
        out_shape=jax.ShapeDtypeStruct((owners, rows, 128), BF16),
        compiler_params=grant(4),
        name="copies",
    )(fields)


def spread_fields(f_ref, o_ref):
    w, blocks, width = f_ref.shape
    fields = f_ref[...].astype(F32)
    lane = lax.broadcasted_iota(jnp.int32, (width, width * RI), 1)
    row = lax.broadcasted_iota(jnp.int32, (width, width * RI), 0)
    repeat = (lane // RI == row).astype(F32).astype(BF16)
    sub = lax.broadcasted_iota(jnp.int32, (RI, width * RI), 0)
    keep = lax.broadcasted_iota(jnp.int32, (RI, width * RI), 1) % RI == sub
    for b in range(blocks):
        v = jnp.dot(fields[:, b, :].astype(BF16), repeat, preferred_element_type=F32)
        e = jnp.where(keep[None], v[:, None, :], 0.0)
        o_ref[:, b * width * RI : (b + 1) * width * RI] = e.reshape(w * RI, width * RI).astype(BF16)


def gen(source, chol, share, first, count):
    vectors, rows, n = chol.shape
    fresh = source.ndim == 3
    w = source.shape[0] if fresh else source.shape[0] // RI
    wb = min(w, WB)
    pieces, ahead = 8, 8
    size = vectors // pieces
    slots = 2 * pieces

    def kernel(s_ref, c_ref, *refs):
        if fresh:
            o_ref, spread_ref, *refs = refs
        else:
            o_ref, *refs = refs
        fk_ref, held, done, acc, in_sems, out_sems, spread_sem = refs
        base = first + share.first_group(rows)

        def fetch(group, piece):
            slot = lax.rem(group, 2) * pieces + piece
            return pltpu.make_async_copy(
                c_ref.at[pl.ds(piece * size, size), pl.ds(pl.multiple_of((base + group) * RI, RI), RI), :],
                held.at[slot],
                in_sems.at[slot],
            )

        def put(group, slot, k):
            at = pl.ds(k * wb, wb)
            return pltpu.make_async_copy(
                done.at[slot, at],
                o_ref.at[at, pl.ds(pl.multiple_of(group * RI, RI), RI), :],
                out_sems.at[slot, k],
            )

        if not fresh:
            spread = pltpu.make_async_copy(s_ref, fk_ref, spread_sem)
            spread.start()

        @pl.loop(0, min(ahead, count * pieces))
        def _(p):
            fetch(p // pieces, lax.rem(p, pieces)).start()

        if fresh:
            spread_fields(s_ref, fk_ref)
            spread = pltpu.make_async_copy(fk_ref, spread_ref, spread_sem)
            spread.start()
        else:
            spread.wait()

        @pl.loop(0, count)
        def _(group):
            side = lax.rem(group, 2)

            @pl.when(group >= 2)
            def _():
                for k in range(w // wb):
                    put(group - 2, side, k).wait()

            for p in range(pieces):
                fetch(group, p).wait()
                later, piece = divmod(p + ahead, pieces)

                @pl.when(group + later < count)
                def _():
                    fetch(group + later, piece).start()

                x = held[side * pieces + p].reshape(size * RI, n)
                for k in range(w // wb):
                    r = slice(k * wb * RI, (k + 1) * wb * RI)
                    part = jnp.dot(fk_ref[r, p * size * RI : (p + 1) * size * RI], x, preferred_element_type=F32)
                    if p == 0:
                        acc[r] = part
                    elif p < pieces - 1:
                        acc[r] += part
                    else:
                        done[side, k * wb : (k + 1) * wb] = (acc[r] + part).reshape(wb, RI, n).astype(BF16)
                        put(group, side, k).start()

        for group in range(max(0, count - 2), count):
            for k in range(w // wb):
                put(group, group % 2, k).wait()
        if fresh:
            spread.wait()

    rows_out = jax.ShapeDtypeStruct((w, count * RI, n), BF16)
    spread_out = jax.ShapeDtypeStruct((w * RI, vectors * RI), BF16)
    out = pl.pallas_call(
        kernel,
        in_specs=[VMEM if fresh else HBM, HBM],
        out_specs=[HBM, HBM] if fresh else HBM,
        out_shape=[rows_out, spread_out] if fresh else rows_out,
        scratch_shapes=[
            pltpu.VMEM((w * RI, vectors * RI), BF16),
            pltpu.VMEM((slots, size, RI, n), BF16),
            pltpu.VMEM((2, w, RI, n), BF16),
            pltpu.VMEM((w * RI, n), F32),
            pltpu.SemaphoreType.DMA((slots,)),
            pltpu.SemaphoreType.DMA((2, w // wb)),
            pltpu.SemaphoreType.DMA,
        ],
        cost_estimate=pl.CostEstimate(
            flops=2 * w * RI * vectors * count * RI * n, bytes_accessed=vectors * count * RI * n * 2, transcendentals=0
        ),
        compiler_params=grant(58),
    )(source, chol)
    return out if fresh else (out, source)


def half(trial, chol):
    vectors, rows, n = chol.shape
    cols = trial.shape[1]
    count = rows // RI

    def kernel(t_ref, x_ref, o_ref):
        x = x_ref[...].reshape(vectors * RI, n)
        p = jnp.dot(x, t_ref[...], preferred_element_type=F32)
        o_ref[...] = p.reshape(o_ref.shape).astype(BF16)

    return pl.pallas_call(
        kernel,
        grid=(count,),
        in_specs=[
            pl.BlockSpec((n, cols), lambda i: (0, 0)),
            pl.BlockSpec((vectors, RI, n), lambda i: (0, i, 0)),
        ],
        out_specs=pl.BlockSpec((vectors, RI, cols), lambda i: (0, 0, i)),
        out_shape=jax.ShapeDtypeStruct((vectors, RI, count * cols), BF16),
        cost_estimate=pl.CostEstimate(
            flops=2 * vectors * count * RI * n * cols,
            bytes_accessed=vectors * count * RI * (n + cols) * 2,
            transcendentals=0,
        ),
        compiler_params=grant(56),
        name="half",
    )(trial, chol)


def taylor_kernel(*refs, counts, parts):
    g_refs = refs[: len(counts)]
    q0_ref, half_ref, send_ref, kept_ref, total, even, odd, sems = refs[len(counts) :]
    piece = kept_ref.shape[0] // sems.shape[0]

    def keep(i):
        at = pl.ds(i * piece, piece)
        return pltpu.make_async_copy(half_ref.at[at], kept_ref.at[at], sems.at[i])

    pl.loop(0, sems.shape[0])(lambda i: keep(i).start())
    n, cols = q0_ref.shape
    nocc = cols // 2
    senders = g_refs[0].shape[0]
    owners = senders // parts
    rows = n // owners
    total[...] = q0_ref[...].astype(F32).reshape(owners, rows, cols)
    source = q0_ref
    for order in range(1, TAYLOR + 1):
        target = (even, odd)[order % 2]
        q = source[...].reshape(n, cols)
        start = 0
        for g_ref, count in zip(g_refs, counts):
            size = count * RI
            for part in range(parts):
                g = g_ref[part * owners : (part + 1) * owners].reshape(owners * size, n)
                p = jnp.dot(g, q, preferred_element_type=F32).reshape(owners, size, cols)
                if order > 1:
                    p = p * (1.0 / order)
                term = jnp.concatenate([-p[:, :, nocc:], p[:, :, :nocc]], axis=2)
                at = part * (rows // parts) + start
                total[:, at : at + size] += term
                if order < TAYLOR:
                    target[:, at : at + size] = term.astype(BF16)
            start += size
        source = target
    fresh = total[...].astype(BF16)
    for b in range(rows // RI):
        send_ref[:, :, b * cols : (b + 1) * cols] = fresh[:, b * RI : (b + 1) * RI]
    pl.loop(0, sems.shape[0])(lambda i: keep(i).wait())


def taylor(received, counts, parts, orbitals, halves):
    kept = (halves.shape[0] // 2,) + halves.shape[1:]
    n, cols = orbitals.shape
    senders = received[0].shape[0]
    owners = senders // parts
    rows = n // owners
    return pl.pallas_call(
        functools.partial(taylor_kernel, counts=counts, parts=parts),
        in_specs=[VMEM] * (len(received) + 1) + [HBM],
        out_specs=[VMEM] * 2,
        out_shape=[
            jax.ShapeDtypeStruct((owners, RI, rows // RI * cols), BF16),
            jax.ShapeDtypeStruct(kept, BF16),
        ],
        scratch_shapes=[
            pltpu.VMEM((owners, rows, cols), F32),
            pltpu.VMEM((owners, rows, cols), BF16),
            pltpu.VMEM((owners, rows, cols), BF16),
            pltpu.SemaphoreType.DMA((8,)),
        ],
        cost_estimate=pl.CostEstimate(flops=2 * TAYLOR * n * n * cols, bytes_accessed=n * (n + 3 * cols) * 2, transcendentals=0),
        compiler_params=grant(36),
        name="taylor",
    )(*received, orbitals, halves)


def bias_kernel(*refs, cols):
    n_ref, s_ref, k_ref, h_ref, o_ref, new_ref, pair, rest, sems, new_sems = refs
    w, _, depth = n_ref.shape
    vectors = h_ref.shape[0]
    wb = min(w, WB)
    nocc = cols // 2
    size = 128
    lanes = wb * 2 * RI
    sub = lax.broadcasted_iota(jnp.int32, (RI, lanes), 0)
    keep = lax.broadcasted_iota(jnp.int32, (RI, lanes), 1) % RI == sub
    kept = k_ref.shape[0]

    def fetch(piece):
        at = pl.ds(piece * size, size)
        return pltpu.make_async_copy(h_ref.at[pl.ds(kept + piece * size, size)], rest.at[at], sems.at[piece])

    def put(group):
        return pltpu.make_async_copy(
            s_ref.at[:, :, pl.ds(pl.multiple_of(group * cols, cols), cols)],
            new_ref.at[:, pl.ds(pl.multiple_of(group * RI, RI), RI), :],
            new_sems.at[group],
        )

    pl.loop(0, (vectors - kept) // size)(lambda piece: fetch(piece).start())
    pl.loop(0, depth // cols)(lambda group: put(group).start())

    def block(k, fetched):
        for s in range(0, depth, cols):
            real = n_ref[pl.ds(k * wb, wb), :, s : s + cols].astype(F32)
            imag = jnp.concatenate([real[:, :, nocc:], -real[:, :, :nocc]], axis=2)
            pair[s : s + cols, :] = jnp.stack([real, imag], axis=1).reshape(lanes, cols).T.astype(BF16)

        def piece(h, v):
            out = jnp.dot(h.reshape(size * RI, depth), pair[...], preferred_element_type=F32)
            out = jnp.where(keep[None], out.reshape(size, RI, lanes), 0.0).sum(axis=1)
            o_ref[pl.ds(k * wb, wb), :, pl.ds(pl.multiple_of(v, size), size)] = (
                out.T.reshape(wb * 2, RI, size).sum(axis=1).reshape(wb, 2, size)
            )

        @pl.loop(0, kept // size)
        def _(i):
            piece(k_ref[pl.ds(i * size, size)], i * size)

        @pl.loop(0, (vectors - kept) // size)
        def _(i):
            if not fetched:
                fetch(i).wait()
            piece(rest[pl.ds(i * size, size)], kept + i * size)

    block(0, False)
    if w > wb:
        pl.loop(1, w // wb)(lambda k: block(k, True))
    pl.loop(0, depth // cols)(lambda group: put(group).wait())


def bias(rows, send, kept, halves, cols):
    w, _, depth = rows.shape
    vectors = halves.shape[0]
    wb = min(w, WB)
    return pl.pallas_call(
        functools.partial(bias_kernel, cols=cols),
        in_specs=[VMEM, VMEM, VMEM, HBM],
        out_specs=[VMEM, HBM],
        out_shape=[
            jax.ShapeDtypeStruct((w, 2, vectors), F32),
            jax.ShapeDtypeStruct((w, depth // cols * RI, cols), BF16),
        ],
        scratch_shapes=[
            pltpu.VMEM((depth, wb * 2 * RI), BF16),
            pltpu.VMEM((vectors - kept.shape[0],) + halves.shape[1:], BF16),
            pltpu.SemaphoreType.DMA(((vectors - kept.shape[0]) // 128,)),
            pltpu.SemaphoreType.DMA((depth // cols,)),
        ],
        cost_estimate=pl.CostEstimate(
            flops=2 * vectors * RI * depth * w * 2 * RI, bytes_accessed=vectors * RI * depth * 2, transcendentals=0
        ),
        compiler_params=grant(40),
        name="bias",
    )(rows, send, kept, halves)


class Share:
    def __init__(self, rows):
        holders = lax.axis_size("groups")
        self.parts = holders if rows // RI % holders == 0 else 1
        self.axes = ("groups", "wide") if self.parts > 1 else "wide"
        self.senders = self.parts * lax.axis_size("wide")

    def first_group(self, rows):
        return lax.axis_index("groups") * (rows // RI // self.parts) if self.parts > 1 else 0


def exchange(v, axes):
    return lax.all_to_all(v, axes, split_axis=0, concat_axis=0, tiled=True)


def splits(groups):
    first = max(1, groups // 4)
    return (first, groups - first) if groups > first else (groups,)


def per_device(fields, chol, orbitals, trial):
    rows = chol.shape[1]
    share = Share(rows)
    counts = splits(rows // RI // share.parts)
    everyone = exchange(copies(fields, share.senders), share.axes)
    source = everyone
    received = []
    start = 0
    for count in counts:
        made, source = gen(source, chol, share, start, count)
        received.append(exchange(made, share.axes))
        start += count
    halves = half(trial, chol)
    send, kept = taylor(received, counts, share.parts, orbitals[0], halves)
    rows_all = exchange(send, "wide")
    partial, fresh = bias(rows_all, send, kept, halves, trial.shape[1])
    mine = exchange(partial, "wide")
    return fresh.reshape(orbitals.shape), mine.sum(axis=0, keepdims=True)


def solution(mesh):
    in_specs = (
        P(("groups", "wide"), None),
        P(None, "wide", None),
        P(("groups", "wide"), None, None),
        P(),
    )
    out_specs = (P(("groups", "wide"), None, None), P(("groups", "wide"), None, None))
    return jax.shard_map(
        per_device, mesh=mesh, in_specs=in_specs, out_specs=out_specs, check_vma=False
    )
```
